512 devices in a mesh: row: 32 (over x, y, core), layer: 16 (over z).
Axes of the slice: x: 4, y: 4, z: 16, core: 2. Of those that a mesh axis runs over, the one named last changes fastest.
Arguments:
- rhs_local: bfloat16 [16, 2, 1024, 256], P('layer', None, 'row'), may hold values from -6 to 6
- dinv_local: bfloat16 [16, 2, 1024, 1024], P('layer', None, 'row')
- lower_anc: bfloat16 [16, 2, 1024, 1024], P('layer', None, 'row'), may hold values from -0.03125 to 0.03125
- lower_high: bfloat16 [16, 2, 32768, 1024], P('layer', None, 'row'), may hold values from -0.046875 to 0.046875
- row_blocks: int32 [16, 2, 256], P('layer', None, 'row'), may hold values from 0 to 15
- rhs_anc: float32 [1024, 256], P('row'), may hold values from -6 to 6
- rhs_high: float32 [65536, 256], P(('row', 'layer')), may hold values from -6 to 6
- dinv_anc: bfloat16 [1024, 1024], P('row')
- lower_anc_high: bfloat16 [65536, 1024], P(('row', 'layer')), may hold values from -0.1875 to 0.1875
Outputs:
- sol_local: bfloat16 [16, 2, 1024, 256], P('layer', None, 'row')
- sol_anc: bfloat16 [1024, 256], P('row')
- high_out: float32 [65536, 256], P(('row', 'layer'))
The draws below stay inside these ranges and needn't reach their ends.
Inputs may be any that keep to these rules, and one draw needn't show every extreme that they name: Row index block q of lower_high, held by row index g = q // 8, lands in block row_blocks of that index's 16 blocks of higher ancestor rows.
All inputs are finite; a program needn't handle non-finite values.
Results may differ from the reference program's by a relative error of at most 0.008.
Values may be sent and summed in bfloat16 or wider, within the bound.
A program may use at most 64 MiB of HBM per device.

```python
import math
import jax
import jax.numpy as jnp
from jax import lax

NS = 1024
RHS = 256
NA = 1024
SN = 2
BLOCK = 128
HBLK = 16
LBLK = 8
N_ROW = 32
N_LAYER = 16


def inverse_blocks(key, shape, order):
    noise = jax.random.normal(key, shape, jnp.float32)
    return jnp.eye(order, dtype=jnp.float32) + 0.6 * noise / math.sqrt(order)


def draw_dinv_local(key, part):
    folded = jax.random.fold_in(key, 11)
    return inverse_blocks(folded, (N_LAYER, SN, NS, NS), NS).astype(jnp.bfloat16)


def draw_dinv_anc(key, part):
    folded = jax.random.fold_in(key, 23)
    return inverse_blocks(folded, (NA, NA), NA).astype(jnp.bfloat16)


def plant(entries, rng, least, top_value):
    spot = [jax.random.randint(jax.random.fold_in(rng, axis), (), 0, length) for axis, length in enumerate(entries.shape)]
    longest = entries.shape.index(max(entries.shape))
    next_to = spot[:longest] + [(spot[longest] + 1) % entries.shape[longest]] + spot[longest + 1:]
    return entries.at[tuple(spot)].set(least).at[tuple(next_to)].set(top_value)


def block_scale(stream_key, dims, cuts, least, high):
    gain = 1.0
    for axis_at, parts in cuts:
        draws = jax.random.uniform(jax.random.fold_in(jax.random.fold_in(stream_key, 6), axis_at), (parts,), jnp.float32, least / len(cuts), high / len(cuts))
        gain = gain * jnp.repeat(jnp.exp(draws), dims[axis_at] // parts).reshape((-1,) + (1,) * (len(dims) - 1 - axis_at))
    return gain


def gaussian(own_key, shape, deviation, bound, split=(), held_as=jnp.bfloat16):
    result = jax.random.normal(own_key, shape, jnp.float32) * deviation
    if len(split) > 0:
        result = block_scale(own_key, shape, split, -0.22, 0.18) * result
    return jnp.clip(result, min=-bound, max=bound).astype(held_as)


def setup_inputs(seed: int = 0) -> dict:
    streams_of = jax.random.split(jax.random.key(seed), 10)
    rhs_local = gaussian(streams_of[0], (N_LAYER, SN, NS, RHS), 1.0, 6.0, ((0, 16), (2, 32)))
    dinv_local = draw_dinv_local(jax.random.fold_in(streams_of[9], 71), 0)
    lower_anc = gaussian(streams_of[2], (N_LAYER, SN, NA, NS), (NS * SN * N_LAYER) ** -0.5, 0.03125, ((0, 16), (2, 32)))
    lower_high = gaussian(streams_of[3], (N_LAYER, SN, N_ROW * LBLK * BLOCK, NS), (NS * N_LAYER) ** -0.5, 0.046875, ((0, 16), (2, 32)))
    row_blocks = plant(jax.random.randint(streams_of[4], (N_LAYER, SN, N_ROW * LBLK), 0, HBLK), jax.random.fold_in(streams_of[4], 1), 0, HBLK - 1).astype(jnp.int32)
    rhs_anc = gaussian(streams_of[5], (NA, RHS), 1.0, 6.0, ((0, 32),), jnp.float32)
    rhs_high = gaussian(streams_of[6], (N_ROW * HBLK * BLOCK, RHS), 1.0, 6.0, ((0, 512),), jnp.float32)
    dinv_anc = draw_dinv_anc(jax.random.fold_in(streams_of[9], 71), 0)
    lower_anc_high = gaussian(streams_of[8], (N_ROW * HBLK * BLOCK, NA), NA ** -0.5, 0.1875, ((0, 512),))
    return dict(rhs_local=rhs_local, dinv_local=dinv_local, lower_anc=lower_anc, lower_high=lower_high, row_blocks=row_blocks, rhs_anc=rhs_anc, rhs_high=rhs_high, dinv_anc=dinv_anc, lower_anc_high=lower_anc_high)


def reference(rhs_local, dinv_local, lower_anc, lower_high, row_blocks, rhs_anc, rhs_high, dinv_anc, lower_anc_high):
    high_total = N_ROW * HBLK * BLOCK
    positions = jnp.arange(N_ROW * LBLK * BLOCK, dtype=jnp.int32)
    owner = (positions // (LBLK * BLOCK)).astype(jnp.int32)
    block_index = (positions // BLOCK).astype(jnp.int32)
    within = (positions % BLOCK).astype(jnp.int32)

    def one_layer(carry, items):
        anc_total, high_sum = carry
        rhs_one, dinv_one, anc_one, high_one, blocks_one = items
        solved = jnp.einsum("sik,skc->sic", dinv_one.astype(jnp.float32), rhs_one.astype(jnp.float32)).astype(jnp.bfloat16)
        solved_wide = solved.astype(jnp.float32)
        anc_total = anc_total + jnp.einsum("sik,skc->ic", anc_one.astype(jnp.float32), solved_wide)
        contrib = jnp.einsum("sik,skc->sic", high_one.astype(jnp.float32), solved_wide)
        targets = (owner[None, :] * (HBLK * BLOCK) + blocks_one[:, block_index] * BLOCK + within[None, :]).astype(jnp.int32)
        high_sum = high_sum.at[targets.reshape(-1)].add(contrib.reshape(-1, RHS))
        return (anc_total, high_sum), solved

    start = (jnp.zeros((NA, RHS), jnp.float32), jnp.zeros((high_total, RHS), jnp.float32))
    (anc_update, high_update), sol_local = lax.scan(one_layer, start, (rhs_local, dinv_local, lower_anc, lower_high, row_blocks))
    anc_rhs = (rhs_anc - anc_update).astype(jnp.bfloat16)
    sol_anc = jnp.dot(dinv_anc, anc_rhs, preferred_element_type=jnp.float32).astype(jnp.bfloat16)
    high_out = rhs_high - high_update - jnp.dot(lower_anc_high, sol_anc, preferred_element_type=jnp.float32)
    return sol_local, sol_anc, high_out
```

```python
import functools

import jax
import jax.numpy as jnp
from jax import lax
from jax.experimental import pallas as pl
from jax.experimental.pallas import tpu as pltpu
from jax.sharding import PartitionSpec as P

BLOCK = 128
HBLK = 16
X, Y, CORES = 4, 4, 2
NEAR_FIRST = (1, 3, 2)
PIECES = 4
STOP = 99


class Copies:
    def __init__(self, send_sem, recv_sem):
        self.send_sem, self.recv_sem = send_sem, recv_sem
        self.used = 0
        self.started = []

    def take(self, count=1):
        first = self.used
        self.used += count
        return first

    def start(self, index, src, dst, device):
        copy = pltpu.make_async_remote_copy(
            src_ref=src,
            dst_ref=dst,
            send_sem=self.send_sem.at[index],
            recv_sem=self.recv_sem.at[index],
            device_id=device,
            device_id_type=pl.DeviceIdType.MESH,
        )
        copy.start()
        self.started.append(copy)

    def arrived(self, index, dst, device):
        pltpu.make_async_remote_copy(
            src_ref=dst,
            dst_ref=dst,
            send_sem=self.send_sem.at[index],
            recv_sem=self.recv_sem.at[index],
            device_id=device,
            device_id_type=pl.DeviceIdType.MESH,
        ).wait_recv()

    def drain(self):
        for copy in self.started:
            copy.wait_send()
        self.started = []


class Place:
    def __init__(self):
        row = lax.axis_index("row")
        self.row = row
        self.x = row // (Y * CORES)
        self.y = (row // CORES) % Y
        self.core = row % CORES

    def at(self, dx, dy, flip=False):
        x = lax.rem(self.x + (dx + X), X)
        y = lax.rem(self.y + (dy + Y), Y)
        core = 1 - self.core if flip else self.core
        return (x * Y + y) * CORES + core


class TreeGather:
    def __init__(self, copies, place, half, both):
        self.copies, self.place, self.half, self.both = copies, place, half, both
        self.first = {(h, d): copies.take() for h in (0, 1) for d in (1, 2, 3)}
        self.second = {
            (h, e, d): copies.take() for h in (0, 1) for e in range(4) for d in (1, 2, 3)
        }
        self.other = {(dx, dy): copies.take() for dx in range(X) for dy in range(Y)}

    def along(self, h, d, e):
        return (d, e) if h == 0 else (e, d)

    def send_first(self, h, d):
        at = self.place.at
        shard = self.half(h, at(0, 0))
        self.copies.start(self.first[h, d], shard, shard, {"row": at(*self.along(h, d, 0))})

    def send_second(self, h, e):
        at = self.place.at
        shard = self.half(h, at(*self.along(h, -e, 0)))
        for d in NEAR_FIRST:
            self.copies.start(
                self.second[h, e, d], shard, shard, {"row": at(*self.along(h, 0, d))}
            )

    def send_other(self, dx, dy):
        at = self.place.at
        shard = self.both(at(-dx, -dy))
        self.copies.start(self.other[dx, dy], shard, shard, {"row": at(0, 0, True)})

    def start(self):
        for d in NEAR_FIRST:
            for h in (0, 1):
                self.send_first(h, d)
        for h in (0, 1):
            self.send_second(h, 0)
        self.send_other(0, 0)

    def finish(self):
        at = self.place.at
        for e in NEAR_FIRST:
            for h in (0, 1):
                self.copies.arrived(
                    self.first[h, e],
                    self.half(h, at(*self.along(h, -e, 0))),
                    {"row": at(*self.along(h, -e, 0))},
                )
                self.send_second(h, e)
        order = [(dx, dy) for dx in range(X) for dy in range(Y) if dx or dy]
        order.sort(key=lambda p: (min(p[0], X - p[0]) + min(p[1], Y - p[1]), p))
        for dx, dy in order:
            source = at(-dx, -dy)
            if dy:
                self.copies.arrived(
                    self.second[0, dx, dy], self.half(0, source), {"row": at(0, -dy)}
                )
            if dx:
                self.copies.arrived(
                    self.second[1, dy, dx], self.half(1, source), {"row": at(-dx, 0)}
                )
            self.send_other(dx, dy)
        for dx, dy in [(0, 0)] + order:
            self.copies.arrived(
                self.other[dx, dy], self.both(at(-dx, -dy, True)), {"row": at(0, 0, True)}
            )


class DirectGather:
    def __init__(self, copies, place, shard):
        self.copies, self.place, self.shard = copies, place, shard
        self.order = [(dx, dy) for dx in range(X) for dy in range(Y) if dx or dy]
        self.order.sort(key=lambda p: (min(p[0], X - p[0]) + min(p[1], Y - p[1]), p))
        self.peer = {p: copies.take() for p in self.order}
        self.other = {p: copies.take() for p in [(0, 0)] + self.order}

    def start(self):
        at = self.place.at
        mine = self.shard(at(0, 0))
        for p in reversed(self.order):
            self.copies.start(self.peer[p], mine, mine, {"row": at(*p)})
        self.send_other(0, 0)

    def send_other(self, dx, dy):
        at = self.place.at
        shard = self.shard(at(-dx, -dy))
        self.copies.start(self.other[dx, dy], shard, shard, {"row": at(0, 0, True)})

    def finish(self):
        at = self.place.at
        for dx, dy in self.order:
            self.copies.arrived(
                self.peer[dx, dy], self.shard(at(-dx, -dy)), {"row": at(-dx, -dy)}
            )
            self.send_other(dx, dy)
        for dx, dy in [(0, 0)] + self.order:
            self.copies.arrived(
                self.other[dx, dy], self.shard(at(-dx, -dy, True)), {"row": at(0, 0, True)}
            )


def dot(a, b):
    return jnp.dot(a, b, preferred_element_type=jnp.float32)


def kernel(
    layers,
    blocks_ref,
    rhs_hbm,
    dinv_hbm,
    anc_hbm,
    high_hbm,
    rhs_anc_hbm,
    rhs_high_hbm,
    dinv_anc_hbm,
    lower_hbm,
    sol_out,
    anc_out,
    high_out,
    dinv,
    anc,
    high,
    rhs_anc,
    rhs_high,
    dinv_anc,
    lower,
    rhs_all,
    sol_all,
    anc_all,
    anc_sol_all,
    partial,
    product,
    up_in,
    up_out,
    down_in,
    down_out,
    anc_near,
    anc_far,
    anc_own,
    result,
    before,
    send_sem,
    recv_sem,
    local_sem,
):
    place = Place()
    row = place.row
    layer = lax.axis_index("layer")
    copies = Copies(send_sem, recv_sem)
    supers, rows, width = sol_out.shape[1:]
    held = supers * blocks_ref.shape[2]
    anc_rows = rhs_anc.shape[0]

    def layer_at(step):
        return lax.rem(layer + (step + layers), layers)

    def span(r, count):
        return pl.ds(pl.multiple_of(r * count, count), count)

    def half_of(ref):
        return lambda h, r: ref.at[h, span(r, rows), :]

    def both_of(ref):
        return lambda r: ref.at[:, span(r, rows), :]

    loads = []
    for n, (src, dst) in enumerate(
        (
            (rhs_hbm.at[0], rhs_all.at[:, span(row, rows), :]),
            (dinv_hbm.at[0], dinv),
            (anc_hbm.at[0], anc),
            (high_hbm.at[0], high),
            (rhs_anc_hbm, rhs_anc),
            (rhs_high_hbm, rhs_high),
            (dinv_anc_hbm, dinv_anc),
            (lower_hbm, lower),
        )
    ):
        load = pltpu.make_async_copy(src, dst, local_sem.at[n])
        load.start()
        loads.append(load)

    barrier = pltpu.get_barrier_semaphore()
    plane = [(dx, dy) for dx in range(X) for dy in range(Y) if dx or dy]
    along = [1, -1, 2, -2, 4, -4, 8]
    for dx, dy in plane:
        pl.semaphore_signal(
            barrier, inc=1, device_id={"row": place.at(dx, dy)}, device_id_type=pl.DeviceIdType.MESH
        )
    pl.semaphore_signal(
        barrier, inc=1, device_id={"row": place.at(0, 0, True)}, device_id_type=pl.DeviceIdType.MESH
    )
    for step in along:
        pl.semaphore_signal(
            barrier, inc=1, device_id={"layer": layer_at(step)}, device_id_type=pl.DeviceIdType.MESH
        )

    home = [blocks_ref[0, i // (held // supers), i % (held // supers)] for i in range(held)]
    for i in range(held):
        last = jnp.int32(held)
        for j in range(i):
            last = jnp.where(home[j] == home[i], j, last)
        before[i] = last
    partial[held] = jnp.zeros_like(partial[held])

    loads[0].wait()
    pl.semaphore_wait(barrier, len(plane) + 1 + len(along))

    gather_rhs = TreeGather(copies, place, half_of(rhs_all), both_of(rhs_all))
    gather_rhs.start()
    gather_rhs.finish()
    loads[1].wait()
    for s in range(supers):
        sol_all[s, span(row, rows), :] = dot(dinv[s], rhs_all[s]).astype(jnp.bfloat16)
    gather_sol = TreeGather(copies, place, half_of(sol_all), both_of(sol_all))
    gather_sol.start()
    store_sol = pltpu.make_async_copy(
        sol_all.at[:, span(row, rows), :], sol_out.at[0], local_sem.at[8]
    )
    store_sol.start()
    gather_sol.finish()

    loads[2].wait()
    own = dot(anc[0], sol_all[0])
    for s in range(1, supers):
        own += dot(anc[s], sol_all[s])
    anc_own[0] = own.astype(jnp.bfloat16)
    near = {step: copies.take() for step in (1, -1, -2)}
    for n, step in enumerate(near):
        copies.start(near[step], anc_own.at[0], anc_near.at[n], {"layer": layer_at(step)})

    loads[3].wait()
    for s in range(supers):
        product[...] = dot(high[s], sol_all[s])
        for q in range(held // supers):
            i = s * (held // supers) + q
            partial[i] = product[q * BLOCK : (q + 1) * BLOCK, :] + partial[before[i]]

    def slot_of(h):
        last = jnp.int32(held)
        for i in range(held):
            last = jnp.where(home[i] == h, i, last)
        return last

    cut = BLOCK // PIECES
    ups, downs = layers // 2, layers // 2 - 1
    up = {(t, p): copies.take() for t in range(ups) for p in range(PIECES)}
    down = {(t, p): copies.take() for t in range(downs) for p in range(PIECES)}

    def reduce_step(t):
        lanes = []
        if t < ups:
            lanes.append((up, up_in, up_out, 1, layer_at(ups - t)))
        if t < downs:
            lanes.append((down, down_in, down_out, -1, layer_at(t - downs)))
        slots = [slot_of(h) for *_, h in lanes]
        for p in range(PIECES):
            piece = pl.ds(p * cut, cut)
            for (index, inbox, outbox, step, _), slot in zip(lanes, slots):
                value = partial[slot, piece, :]
                if t:
                    copies.arrived(
                        index[t - 1, p], inbox.at[t - 1, piece, :], {"layer": layer_at(-step)}
                    )
                    value = value + inbox[t - 1, piece, :].astype(jnp.float32)
                outbox[t, piece, :] = value.astype(jnp.bfloat16)
                copies.start(
                    index[t, p],
                    outbox.at[t, piece, :],
                    inbox.at[t, piece, :],
                    {"layer": layer_at(step)},
                )

    reduce_step(0)

    for n, step in enumerate(near):
        copies.arrived(near[step], anc_near.at[n], {"layer": layer_at(-step)})
        own = own + anc_near[n].astype(jnp.float32)
    anc_own[1] = own.astype(jnp.bfloat16)
    far = {step: copies.take() for step in (8, 4, -4)}
    for n, step in enumerate(far):
        copies.start(far[step], anc_own.at[1], anc_far.at[n], {"layer": layer_at(step)})

    for t in (1, 2, 3):
        reduce_step(t)

    for n, step in enumerate(far):
        copies.arrived(far[step], anc_far.at[n], {"layer": layer_at(-step)})
        own = own + anc_far[n].astype(jnp.float32)
    loads[4].wait()
    anc_all[span(row, anc_rows), :] = (rhs_anc[...] - own).astype(jnp.bfloat16)
    gather_anc = DirectGather(copies, place, lambda r: anc_all.at[span(r, anc_rows), :])
    gather_anc.start()
    for t in (4, 5):
        reduce_step(t)
    gather_anc.finish()
    loads[6].wait()
    anc_sol_all[span(row, anc_rows), :] = dot(dinv_anc[...], anc_all[...]).astype(jnp.bfloat16)
    gather_out = DirectGather(copies, place, lambda r: anc_sol_all.at[span(r, anc_rows), :])
    gather_out.start()
    store_anc = pltpu.make_async_copy(
        anc_sol_all.at[span(row, anc_rows), :], anc_out, local_sem.at[9]
    )
    store_anc.start()
    for t in range(6, ups):
        reduce_step(t)
    loads[5].wait()
    slot = slot_of(layer)
    for p in range(PIECES):
        piece = pl.ds(p * cut, cut)
        copies.arrived(up[ups - 1, p], up_in.at[ups - 1, piece, :], {"layer": layer_at(-1)})
        copies.arrived(down[downs - 1, p], down_in.at[downs - 1, piece, :], {"layer": layer_at(1)})
        summed = partial[slot, piece, :] + up_in[ups - 1, piece, :].astype(jnp.float32)
        summed = summed + down_in[downs - 1, piece, :].astype(jnp.float32)
        result[piece, :] = rhs_high[piece, :] - summed
    gather_out.finish()
    loads[7].wait()
    result[...] = result[...] - dot(lower[...], anc_sol_all[...])
    store_high = pltpu.make_async_copy(result, high_out, local_sem.at[10])
    store_high.start()
    copies.drain()
    store_sol.wait()
    store_anc.wait()
    store_high.wait()


def on_device(layers, rhs_local, dinv_local, lower_anc, lower_high, row_blocks, rhs_anc, rhs_high, dinv_anc, lower_anc_high):
    supers, rows, width = rhs_local.shape[1:]
    order = dinv_local.shape[3]
    anc_rows, anc_order = dinv_anc.shape
    held = supers * row_blocks.shape[2]
    bf16, f32 = jnp.bfloat16, jnp.float32
    anywhere = pl.BlockSpec(memory_space=pl.ANY)
    half = layers // 2
    return pl.pallas_call(
        functools.partial(kernel, layers),
        out_shape=(
            jax.ShapeDtypeStruct(rhs_local.shape, bf16),
            jax.ShapeDtypeStruct(rhs_anc.shape, bf16),
            jax.ShapeDtypeStruct(rhs_high.shape, f32),
        ),
        in_specs=[pl.BlockSpec(memory_space=pltpu.SMEM)] + [anywhere] * 8,
        out_specs=(anywhere,) * 3,
        scratch_shapes=[
            pltpu.VMEM(dinv_local.shape[1:], bf16),
            pltpu.VMEM(lower_anc.shape[1:], bf16),
            pltpu.VMEM(lower_high.shape[1:], bf16),
            pltpu.VMEM(rhs_anc.shape, f32),
            pltpu.VMEM(rhs_high.shape, f32),
            pltpu.VMEM(dinv_anc.shape, bf16),
            pltpu.VMEM(lower_anc_high.shape, bf16),
            pltpu.VMEM((supers, order, width), bf16),
            pltpu.VMEM((supers, order, width), bf16),
            pltpu.VMEM((anc_order, width), bf16),
            pltpu.VMEM((anc_order, width), bf16),
            pltpu.VMEM((held + 1, BLOCK, width), f32),
            pltpu.VMEM((lower_high.shape[2], width), f32),
            pltpu.VMEM((half, BLOCK, width), bf16),
            pltpu.VMEM((half, BLOCK, width), bf16),
            pltpu.VMEM((half, BLOCK, width), bf16),
            pltpu.VMEM((half, BLOCK, width), bf16),
            pltpu.VMEM((3, anc_rows, width), bf16),
            pltpu.VMEM((3, anc_rows, width), bf16),
            pltpu.VMEM((2, anc_rows, width), bf16),
            pltpu.VMEM(rhs_high.shape, f32),
            pltpu.SMEM((held,), jnp.int32),
            pltpu.SemaphoreType.DMA((256,)),
            pltpu.SemaphoreType.DMA((256,)),
            pltpu.SemaphoreType.DMA((11,)),
        ],
        compiler_params=pltpu.CompilerParams(collective_id=0, has_side_effects=True),
    )(row_blocks, rhs_local, dinv_local, lower_anc, lower_high, rhs_anc, rhs_high, dinv_anc, lower_anc_high)


def solution(mesh):
    return jax.shard_map(
        functools.partial(on_device, mesh.shape["layer"]),
        mesh=mesh,
        in_specs=(
            P("layer", None, "row", None),
            P("layer", None, "row", None),
            P("layer", None, "row", None),
            P("layer", None, "row", None),
            P("layer", None, "row"),
            P("row", None),
            P(("row", "layer"), None),
            P("row", None),
            P(("row", "layer"), None),
        ),
        out_specs=(P("layer", None, "row", None), P("row", None), P(("row", "layer"), None)),
        check_vma=False,
    )
```

```python
import functools

import jax
import jax.numpy as jnp
from jax import lax
from jax.experimental import pallas as pl
from jax.experimental.pallas import tpu as pltpu
from jax.sharding import PartitionSpec as P

BLOCK = 128
HBLK = 16
X, Y, CORES = 4, 4, 2
NEAR_FIRST = (1, 3, 2)
PIECES = 2


class Copies:
    def __init__(self, send_sem, recv_sem):
        self.send_sem, self.recv_sem = send_sem, recv_sem
        self.used = 0
        self.started = []

    def take(self, count=1):
        first = self.used
        self.used += count
        return first

    def start(self, index, src, dst, device):
        copy = pltpu.make_async_remote_copy(
            src_ref=src,
            dst_ref=dst,
            send_sem=self.send_sem.at[index],
            recv_sem=self.recv_sem.at[index],
            device_id=device,
            device_id_type=pl.DeviceIdType.MESH,
        )
        copy.start()
        self.started.append(copy)

    def arrived(self, index, dst, device):
        pltpu.make_async_remote_copy(
            src_ref=dst,
            dst_ref=dst,
            send_sem=self.send_sem.at[index],
            recv_sem=self.recv_sem.at[index],
            device_id=device,
            device_id_type=pl.DeviceIdType.MESH,
        ).wait_recv()

    def drain(self):
        for copy in self.started:
            copy.wait_send()
        self.started = []


class Place:
    def __init__(self):
        row = lax.axis_index("row")
        self.row = row
        self.x = row // (Y * CORES)
        self.y = (row // CORES) % Y
        self.core = row % CORES

    def at(self, dx, dy, flip=False):
        x = lax.rem(self.x + (dx + X), X)
        y = lax.rem(self.y + (dy + Y), Y)
        core = 1 - self.core if flip else self.core
        return (x * Y + y) * CORES + core


class TreeGather:
    def __init__(self, copies, place, half, both):
        self.copies, self.place, self.half, self.both = copies, place, half, both
        self.first = {(h, d): copies.take() for h in (0, 1) for d in (1, 2, 3)}
        self.second = {
            (h, e, d): copies.take() for h in (0, 1) for e in range(4) for d in (1, 2, 3)
        }
        self.other = {(dx, dy): copies.take() for dx in range(X) for dy in range(Y)}

    def along(self, h, d, e):
        return (d, e) if h == 0 else (e, d)

    def send_first(self, h, d):
        at = self.place.at
        shard = self.half(h, at(0, 0))
        self.copies.start(self.first[h, d], shard, shard, {"row": at(*self.along(h, d, 0))})

    def send_second(self, h, e):
        at = self.place.at
        shard = self.half(h, at(*self.along(h, -e, 0)))
        for d in NEAR_FIRST:
            self.copies.start(
                self.second[h, e, d], shard, shard, {"row": at(*self.along(h, 0, d))}
            )

    def send_other(self, dx, dy):
        at = self.place.at
        shard = self.both(at(-dx, -dy))
        self.copies.start(self.other[dx, dy], shard, shard, {"row": at(0, 0, True)})

    def start(self):
        for d in NEAR_FIRST:
            for h in (0, 1):
                self.send_first(h, d)
        for h in (0, 1):
            self.send_second(h, 0)
        self.send_other(0, 0)

    def finish(self):
        at = self.place.at
        for e in NEAR_FIRST:
            for h in (0, 1):
                self.copies.arrived(
                    self.first[h, e],
                    self.half(h, at(*self.along(h, -e, 0))),
                    {"row": at(*self.along(h, -e, 0))},
                )
                self.send_second(h, e)
        order = [(dx, dy) for dx in range(X) for dy in range(Y) if dx or dy]
        order.sort(key=lambda p: (min(p[0], X - p[0]) + min(p[1], Y - p[1]), p))
        for dx, dy in order:
            source = at(-dx, -dy)
            if dy:
                self.copies.arrived(
                    self.second[0, dx, dy], self.half(0, source), {"row": at(0, -dy)}
                )
            if dx:
                self.copies.arrived(
                    self.second[1, dy, dx], self.half(1, source), {"row": at(-dx, 0)}
                )
            self.send_other(dx, dy)
        for dx, dy in [(0, 0)] + order:
            self.copies.arrived(
                self.other[dx, dy], self.both(at(-dx, -dy, True)), {"row": at(0, 0, True)}
            )


class DirectGather:
    def __init__(self, copies, place, shard):
        self.copies, self.place, self.shard = copies, place, shard
        self.order = [(dx, dy) for dx in range(X) for dy in range(Y) if dx or dy]
        self.order.sort(key=lambda p: (min(p[0], X - p[0]) + min(p[1], Y - p[1]), p))
        self.peer = {p: copies.take() for p in self.order}
        self.other = {p: copies.take() for p in [(0, 0)] + self.order}

    def start(self):
        at = self.place.at
        mine = self.shard(at(0, 0))
        for p in reversed(self.order):
            self.copies.start(self.peer[p], mine, mine, {"row": at(*p)})
        self.send_other(0, 0)

    def send_other(self, dx, dy):
        at = self.place.at
        shard = self.shard(at(-dx, -dy))
        self.copies.start(self.other[dx, dy], shard, shard, {"row": at(0, 0, True)})

    def finish(self):
        at = self.place.at
        for dx, dy in self.order:
            self.copies.arrived(
                self.peer[dx, dy], self.shard(at(-dx, -dy)), {"row": at(-dx, -dy)}
            )
            self.send_other(dx, dy)
        for dx, dy in [(0, 0)] + self.order:
            self.copies.arrived(
                self.other[dx, dy], self.shard(at(-dx, -dy, True)), {"row": at(0, 0, True)}
            )


def dot(a, b):
    return jnp.dot(a, b, preferred_element_type=jnp.float32)


def kernel(
    layers,
    blocks_ref,
    rhs_hbm,
    dinv_hbm,
    anc_hbm,
    high_hbm,
    rhs_anc_hbm,
    rhs_high_hbm,
    dinv_anc_hbm,
    lower_hbm,
    sol_out,
    anc_out,
    high_out,
    dinv,
    anc,
    high,
    rhs_anc,
    rhs_high,
    dinv_anc_all,
    lower,
    rhs_all,
    sol_all,
    anc_all,
    anc_sol,
    partial,
    product,
    reach,
    chain_in,
    chain_out,
    side_in,
    side_out,
    anc_near,
    anc_far,
    anc_own,
    result,
    before,
    send_sem,
    recv_sem,
    local_sem,
    relay,
):
    place = Place()
    row = place.row
    layer = lax.axis_index("layer")
    copies = Copies(send_sem, recv_sem)
    supers, rows, width = sol_out.shape[1:]
    held = supers * blocks_ref.shape[2]
    anc_rows = rhs_anc.shape[0]

    def layer_at(step):
        return lax.rem(layer + (step + layers), layers)

    def signal(sem, where):
        pl.semaphore_signal(sem, inc=1, device_id=where, device_id_type=pl.DeviceIdType.MESH)

    def span(r, count):
        return pl.ds(pl.multiple_of(r * count, count), count)

    def half_of(ref):
        return lambda h, r: ref.at[h, span(r, rows), :]

    def both_of(ref):
        return lambda r: ref.at[:, span(r, rows), :]

    loads = []
    for n, (src, dst) in enumerate(
        (
            (rhs_hbm.at[0], rhs_all.at[:, span(row, rows), :]),
            (dinv_hbm.at[0], dinv),
            (anc_hbm.at[0], anc),
            (high_hbm.at[0], high),
            (rhs_anc_hbm, rhs_anc),
            (rhs_high_hbm, rhs_high),
            (dinv_anc_hbm, dinv_anc_all.at[span(row, anc_rows), :]),
            (lower_hbm, lower),
        )
    ):
        load = pltpu.make_async_copy(src, dst, local_sem.at[n])
        load.start()
        loads.append(load)

    barrier = pltpu.get_barrier_semaphore()
    plane = [(dx, dy) for dx in range(X) for dy in range(Y) if dx or dy]
    along = [1, -1, 2, -2]
    for step in along:
        signal(barrier, {"layer": layer_at(step)})
    for dx, dy in plane:
        signal(barrier, {"row": place.at(dx, dy)})
    signal(barrier, {"row": place.at(0, 0, True)})

    home = [blocks_ref[0, i // (held // supers), i % (held // supers)] for i in range(held)]
    for i in range(held):
        last = jnp.int32(held)
        for j in range(i):
            last = jnp.where(home[j] == home[i], j, last)
        before[i] = last
    partial[held] = jnp.zeros_like(partial[held])

    loads[0].wait()
    pl.semaphore_wait(barrier, len(plane) + 1 + len(along))
    for step in (2, -2):
        signal(relay.at[0], {"layer": layer_at(step)})

    gather_rhs = TreeGather(copies, place, half_of(rhs_all), both_of(rhs_all))
    gather_rhs.start()
    gather_rhs.finish()
    pl.semaphore_wait(relay.at[0], 2)
    signal(relay.at[1], {"layer": layer_at(-4)})
    loads[1].wait()
    for s in range(supers):
        sol_all[s, span(row, rows), :] = dot(dinv[s], rhs_all[s]).astype(jnp.bfloat16)
    gather_sol = TreeGather(copies, place, half_of(sol_all), both_of(sol_all))
    gather_sol.start()
    store_sol = pltpu.make_async_copy(
        sol_all.at[:, span(row, rows), :], sol_out.at[0], local_sem.at[8]
    )
    store_sol.start()
    gather_sol.finish()
    pl.semaphore_wait(relay.at[1], 1)

    loads[2].wait()
    own = dot(anc[0], sol_all[0])
    for s in range(1, supers):
        own += dot(anc[s], sol_all[s])
    anc_own[0] = own.astype(jnp.bfloat16)
    near = {step: copies.take() for step in (1, -1, -2)}
    for n, step in enumerate(near):
        copies.start(near[step], anc_own.at[0], anc_near.at[n], {"layer": layer_at(step)})
    loads[6].wait()
    gather_dinv = DirectGather(copies, place, lambda r: dinv_anc_all.at[span(r, anc_rows), :])
    gather_dinv.start()

    loads[3].wait()
    for s in range(supers):
        product[...] = dot(high[s], sol_all[s])
        for q in range(held // supers):
            i = s * (held // supers) + q
            partial[i] = product[q * BLOCK : (q + 1) * BLOCK, :] + partial[before[i]]

    def slot_of(h):
        last = jnp.int32(held)
        for i in range(held):
            last = jnp.where(home[i] == h, i, last)
        return last

    cut = BLOCK // PIECES
    ways = (1, -1)
    far_half = {1: range(0, PIECES // 2), -1: range(PIECES // 2, PIECES)}
    chain = {(w, d, p): copies.take() for w in ways for d in (8, 6, 4, 2) for p in range(PIECES)}
    side = {(w, d): copies.take() for w in ways for d in (7, 5, 3, 1)}

    def box(w, n):
        return n if w == 1 else n + 4

    def send_chain(w, d, p, value):
        piece = pl.ds(p * cut, cut)
        at = box(w, d // 2 - 1)
        chain_out[at, piece, :] = value.astype(jnp.bfloat16)
        copies.start(
            chain[w, d, p],
            chain_out.at[at, piece, :],
            chain_in.at[at, piece, :],
            {"layer": layer_at(2 * w)},
        )

    def send_sides(d):
        for w in ways:
            at = box(w, d // 2)
            side_out[at] = partial[slot_of(layer_at(w * d))].astype(jnp.bfloat16)
            copies.start(side[w, d], side_out.at[at], side_in.at[at], {"layer": layer_at(w)})

    def arrived(w, d, p, value, fresh):
        piece = pl.ds(p * cut, cut)
        if d + 2 < 8 or p in far_half[w]:
            at = box(w, d // 2)
            copies.arrived(
                chain[w, d + 2, p], chain_in.at[at, piece, :], {"layer": layer_at(-2 * w)}
            )
            value = value + chain_in[at, piece, :].astype(jnp.float32)
        at = box(w, d // 2)
        if fresh:
            copies.arrived(side[w, d + 1], side_in.at[at], {"layer": layer_at(-w)})
        return value + side_in[at, piece, :].astype(jnp.float32)

    def pass_on(d):
        slots = {w: slot_of(layer_at(w * d)) for w in ways}
        for p in range(PIECES):
            piece = pl.ds(p * cut, cut)
            for w in ways:
                value = arrived(w, d, p, partial[slots[w], piece, :], p == 0)
                send_chain(w, d, p, value)

    for n, step in enumerate(near):
        copies.arrived(near[step], anc_near.at[n], {"layer": layer_at(-step)})
        own = own + anc_near[n].astype(jnp.float32)
    anc_own[1] = own.astype(jnp.bfloat16)
    far = {step: copies.take() for step in (8, 4, -4)}
    for n, step in enumerate(far):
        copies.start(far[step], anc_own.at[1], anc_far.at[n], {"layer": layer_at(step)})

    slot = slot_of(layer_at(8))
    for w in ways:
        for p in far_half[w]:
            send_chain(w, 8, p, partial[slot, pl.ds(p * cut, cut), :])
    send_sides(7)
    send_sides(5)
    pass_on(6)
    send_sides(3)

    for n, step in enumerate(far):
        copies.arrived(far[step], anc_far.at[n], {"layer": layer_at(-step)})
        own = own + anc_far[n].astype(jnp.float32)
    loads[4].wait()
    anc_all[span(row, anc_rows), :] = (rhs_anc[...] - own).astype(jnp.bfloat16)
    gather_anc = DirectGather(copies, place, lambda r: anc_all.at[span(r, anc_rows), :])
    gather_anc.start()
    pass_on(4)
    send_sides(1)
    gather_dinv.finish()
    loads[7].wait()
    spread = dot(lower[...], dinv_anc_all[...])
    reach[0] = spread.astype(jnp.bfloat16)
    reach[1] = (spread - reach[0].astype(jnp.float32)).astype(jnp.bfloat16)
    pass_on(2)
    gather_anc.finish()
    anc_sol[...] = dot(dinv_anc_all[span(row, anc_rows), :], anc_all[...]).astype(jnp.bfloat16)
    store_anc = pltpu.make_async_copy(anc_sol, anc_out, local_sem.at[9])
    store_anc.start()
    loads[5].wait()
    result[...] = rhs_high[...] - dot(reach[0], anc_all[...]) - dot(reach[1], anc_all[...])
    slot = slot_of(layer)
    for p in range(PIECES):
        piece = pl.ds(p * cut, cut)
        summed = partial[slot, piece, :]
        for w in ways:
            summed = arrived(w, 0, p, summed, p == 0)
        result[piece, :] = result[piece, :] - summed
    store_high = pltpu.make_async_copy(result, high_out, local_sem.at[10])
    store_high.start()
    copies.drain()
    store_sol.wait()
    store_anc.wait()
    store_high.wait()


def hand_over(*refs):
    count = len(refs) // 3
    given, wanted, held = refs[:count], refs[count : 2 * count], refs[2 * count : -1]
    sem = refs[-1]
    loads = [pltpu.make_async_copy(a, b, sem.at[0, n]) for n, (a, b) in enumerate(zip(given, held))]
    stores = [pltpu.make_async_copy(a, b, sem.at[1, n]) for n, (a, b) in enumerate(zip(held, wanted))]
    for load in loads:
        load.start()
    for load, store in zip(loads, stores):
        load.wait()
        store.start()
    for store in stores:
        store.wait()


def on_device(layers, rhs_local, dinv_local, lower_anc, lower_high, row_blocks, rhs_anc, rhs_high, dinv_anc, lower_anc_high):
    supers, rows, width = rhs_local.shape[1:]
    order = dinv_local.shape[3]
    anc_rows, anc_order = dinv_anc.shape
    held = supers * row_blocks.shape[2]
    bf16, f32 = jnp.bfloat16, jnp.float32
    anywhere = pl.BlockSpec(memory_space=pl.ANY)
    shapes = (
        jax.ShapeDtypeStruct(rhs_local.shape, bf16),
        jax.ShapeDtypeStruct(rhs_anc.shape, bf16),
        jax.ShapeDtypeStruct(rhs_high.shape, f32),
    )
    outs = pl.pallas_call(
        functools.partial(kernel, layers),
        out_shape=shapes,
        in_specs=[pl.BlockSpec(memory_space=pltpu.SMEM)] + [anywhere] * 8,
        out_specs=(anywhere,) * 3,
        scratch_shapes=[
            pltpu.VMEM(dinv_local.shape[1:], bf16),
            pltpu.VMEM(lower_anc.shape[1:], bf16),
            pltpu.VMEM(lower_high.shape[1:], bf16),
            pltpu.VMEM(rhs_anc.shape, f32),
            pltpu.VMEM(rhs_high.shape, f32),
            pltpu.VMEM((anc_order, anc_order), bf16),
            pltpu.VMEM(lower_anc_high.shape, bf16),
            pltpu.VMEM((supers, order, width), bf16),
            pltpu.VMEM((supers, order, width), bf16),
            pltpu.VMEM((anc_order, width), bf16),
            pltpu.VMEM((anc_rows, width), bf16),
            pltpu.VMEM((held + 1, BLOCK, width), f32),
            pltpu.VMEM((lower_high.shape[2], width), f32),
            pltpu.VMEM((2, BLOCK, anc_order), bf16),
            pltpu.VMEM((8, BLOCK, width), bf16),
            pltpu.VMEM((8, BLOCK, width), bf16),
            pltpu.VMEM((8, BLOCK, width), bf16),
            pltpu.VMEM((8, BLOCK, width), bf16),
            pltpu.VMEM((3, anc_rows, width), bf16),
            pltpu.VMEM((3, anc_rows, width), bf16),
            pltpu.VMEM((2, anc_rows, width), bf16),
            pltpu.VMEM(rhs_high.shape, f32),
            pltpu.SMEM((held,), jnp.int32),
            pltpu.SemaphoreType.DMA((256,)),
            pltpu.SemaphoreType.DMA((256,)),
            pltpu.SemaphoreType.DMA((11,)),
            pltpu.SemaphoreType.REGULAR((2,)),
        ],
        compiler_params=pltpu.CompilerParams(collective_id=0, has_side_effects=True),
    )(row_blocks, rhs_local, dinv_local, lower_anc, lower_high, rhs_anc, rhs_high, dinv_anc, lower_anc_high)
    return pl.pallas_call(
        hand_over,
        out_shape=shapes,
        in_specs=[anywhere] * 3,
        out_specs=(anywhere,) * 3,
        scratch_shapes=[pltpu.VMEM(a.shape, a.dtype) for a in shapes]
        + [pltpu.SemaphoreType.DMA((2, 3))],
    )(*outs)


def solution(mesh):
    return jax.shard_map(
        functools.partial(on_device, mesh.shape["layer"]),
        mesh=mesh,
        in_specs=(
            P("layer", None, "row", None),
            P("layer", None, "row", None),
            P("layer", None, "row", None),
            P("layer", None, "row", None),
            P("layer", None, "row"),
            P("row", None),
            P(("row", "layer"), None),
            P("row", None),
            P(("row", "layer"), None),
        ),
        out_specs=(P("layer", None, "row", None), P("row", None), P(("row", "layer"), None)),
        check_vma=False,
    )
```

```python
import functools

import jax
import jax.numpy as jnp
from jax import lax
from jax.experimental import pallas as pl
from jax.experimental.pallas import tpu as pltpu
from jax.sharding import PartitionSpec as P

BLOCK = 128
HBLK = 16
X, Y, CORES = 4, 4, 2
PIECES = 2


class Copies:
    def __init__(self, send_sem, recv_sem):
        self.send_sem, self.recv_sem = send_sem, recv_sem
        self.used = 0
        self.started = []

    def take(self, count=1):
        first = self.used
        self.used += count
        return first

    def start(self, index, src, dst, device):
        copy = pltpu.make_async_remote_copy(
            src_ref=src,
            dst_ref=dst,
            send_sem=self.send_sem.at[index],
            recv_sem=self.recv_sem.at[index],
            device_id=device,
            device_id_type=pl.DeviceIdType.MESH,
        )
        copy.start()
        self.started.append(copy)

    def arrived(self, index, dst, device):
        pltpu.make_async_remote_copy(
            src_ref=dst,
            dst_ref=dst,
            send_sem=self.send_sem.at[index],
            recv_sem=self.recv_sem.at[index],
            device_id=device,
            device_id_type=pl.DeviceIdType.MESH,
        ).wait_recv()

    def drain(self):
        for copy in self.started:
            copy.wait_send()
        self.started = []


class Place:
    def __init__(self):
        row = lax.axis_index("row")
        self.row = row
        self.x = row // (Y * CORES)
        self.y = (row // CORES) % Y
        self.core = row % CORES

    def at(self, dx, dy, flip=False):
        x = lax.rem(self.x + (dx + X), X)
        y = lax.rem(self.y + (dy + Y), Y)
        core = 1 - self.core if flip else self.core
        return (x * Y + y) * CORES + core


class TreeGather:
    def __init__(self, copies, place, half, both):
        self.copies, self.place, self.half, self.both = copies, place, half, both
        self.order = [(dx, dy) for dx in range(X) for dy in range(Y) if dx or dy]
        self.order.sort(key=lambda p: (min(p[0], X - p[0]) + min(p[1], Y - p[1]), p))
        self.first = {(h, d): copies.take() for h in (0, 1) for d in (1, 2, 3)}
        self.second = {
            (h, e, d): copies.take() for h in (0, 1) for e in range(4) for d in (1, 2, 3)
        }
        self.other = {(dx, dy): copies.take() for dx in range(X) for dy in range(Y)}

    def along(self, h, d, e):
        return (d, e) if h == 0 else (e, d)

    def send_first(self, h, d):
        at = self.place.at
        shard = self.half(h, at(0, 0))
        self.copies.start(self.first[h, d], shard, shard, {"row": at(*self.along(h, d, 0))})

    def send_second(self, h, e):
        at = self.place.at
        shard = self.half(h, at(*self.along(h, -e, 0)))
        for d in (1, 3, 2):
            self.copies.start(
                self.second[h, e, d], shard, shard, {"row": at(*self.along(h, 0, d))}
            )

    def send_other(self, dx, dy):
        at = self.place.at
        shard = self.both(at(-dx, -dy))
        self.copies.start(self.other[dx, dy], shard, shard, {"row": at(0, 0, True)})

    def start(self):
        for d in (1, 3, 2):
            for h in (0, 1):
                self.send_first(h, d)
        for h in (0, 1):
            self.send_second(h, 0)
        self.send_other(0, 0)

    def turn(self):
        at = self.place.at
        for e in (1, 3, 2):
            for h in (0, 1):
                self.copies.arrived(
                    self.first[h, e],
                    self.half(h, at(*self.along(h, -e, 0))),
                    {"row": at(*self.along(h, -e, 0))},
                )
                self.send_second(h, e)

    def forward(self):
        at = self.place.at
        for dx, dy in self.order:
            source = at(-dx, -dy)
            if dy:
                self.copies.arrived(
                    self.second[0, dx, dy], self.half(0, source), {"row": at(0, -dy)}
                )
            if dx:
                self.copies.arrived(
                    self.second[1, dy, dx], self.half(1, source), {"row": at(-dx, 0)}
                )
            self.send_other(dx, dy)

    def complete(self):
        at = self.place.at
        for dx, dy in [(0, 0)] + self.order:
            self.copies.arrived(
                self.other[dx, dy], self.both(at(-dx, -dy, True)), {"row": at(0, 0, True)}
            )


class DirectGather:
    def __init__(self, copies, place, shard):
        self.copies, self.place, self.shard = copies, place, shard
        self.order = [(dx, dy) for dx in range(X) for dy in range(Y) if dx or dy]
        self.order.sort(key=lambda p: (min(p[0], X - p[0]) + min(p[1], Y - p[1]), p))
        self.peer = {p: copies.take() for p in self.order}
        self.other = {p: copies.take() for p in [(0, 0)] + self.order}

    def start(self):
        at = self.place.at
        mine = self.shard(at(0, 0))
        for p in reversed(self.order):
            self.copies.start(self.peer[p], mine, mine, {"row": at(*p)})
        self.send_other(0, 0)

    def send_other(self, dx, dy):
        at = self.place.at
        shard = self.shard(at(-dx, -dy))
        self.copies.start(self.other[dx, dy], shard, shard, {"row": at(0, 0, True)})

    def forward(self):
        at = self.place.at
        for dx, dy in self.order:
            self.copies.arrived(
                self.peer[dx, dy], self.shard(at(-dx, -dy)), {"row": at(-dx, -dy)}
            )
            self.send_other(dx, dy)

    def complete(self):
        at = self.place.at
        for dx, dy in [(0, 0)] + self.order:
            self.copies.arrived(
                self.other[dx, dy], self.shard(at(-dx, -dy, True)), {"row": at(0, 0, True)}
            )


def dot(a, b):
    return jnp.dot(a, b, preferred_element_type=jnp.float32)


def kernel(
    layers,
    blocks_hbm,
    rhs_hbm,
    dinv_hbm,
    anc_hbm,
    high_hbm,
    rhs_anc_hbm,
    rhs_high_hbm,
    dinv_anc_hbm,
    lower_hbm,
    sol_out,
    anc_out,
    high_out,
    dinv,
    anc,
    high,
    rhs_anc,
    rhs_high,
    dinv_anc_all,
    lower,
    rhs_all,
    sol_all,
    anc_all,
    anc_sol,
    partial,
    product,
    reach,
    chain_in,
    chain_out,
    side_in,
    side_out,
    anc_near,
    anc_far,
    anc_own,
    result,
    blocks_ref,
    before,
    final,
    send_sem,
    recv_sem,
    local_sem,
    relay,
):
    place = Place()
    row = place.row
    layer = lax.axis_index("layer")
    copies = Copies(send_sem, recv_sem)
    supers, rows, width = sol_out.shape[1:]
    held = supers * blocks_ref.shape[2]
    anc_rows = rhs_anc.shape[0]

    def layer_at(step):
        return lax.rem(layer + (step + layers), layers)

    def signal(sem, where):
        pl.semaphore_signal(sem, inc=1, device_id=where, device_id_type=pl.DeviceIdType.MESH)

    def span(r, count):
        return pl.ds(pl.multiple_of(r * count, count), count)

    def shards_of(ref, s):
        return lambda r: ref.at[s, span(r, rows), :]

    loads = []
    for n, (src, dst) in enumerate(
        (
            (rhs_hbm.at[0], rhs_all.at[:, span(row, rows), :]),
            (dinv_hbm.at[0], dinv),
            (anc_hbm.at[0], anc),
            (high_hbm.at[0], high),
            (rhs_anc_hbm, rhs_anc),
            (rhs_high_hbm, rhs_high),
            (dinv_anc_hbm, dinv_anc_all.at[span(row, anc_rows), :]),
            (lower_hbm, lower),
            (blocks_hbm, blocks_ref),
        )
    ):
        load = pltpu.make_async_copy(src, dst, local_sem.at[n])
        load.start()
        loads.append(load)

    barrier = pltpu.get_barrier_semaphore()
    lines = [(d, 0) for d in (2, 1, 3)] + [(0, d) for d in (2, 1, 3)]
    along = [1, -1, 2, -2]
    for step in along:
        signal(barrier, {"layer": layer_at(step)})
    for dx, dy in lines:
        signal(barrier, {"row": place.at(dx, dy)})
    signal(barrier, {"row": place.at(0, 0, True)})

    loads[0].wait()
    pl.semaphore_wait(barrier, len(lines) + 1 + len(along))
    for step in (2, -2):
        signal(relay.at[0], {"layer": layer_at(step)})

    gather_rhs = TreeGather(
        copies,
        place,
        lambda h, r: rhs_all.at[h, span(r, rows), :],
        lambda r: rhs_all.at[:, span(r, rows), :],
    )
    gather_rhs.start()
    loads[8].wait()
    home = [blocks_ref[0, i // (held // supers), i % (held // supers)] for i in range(held)]
    for i in range(held):
        last = jnp.int32(held)
        for j in range(i):
            last = jnp.where(home[j] == home[i], j, last)
        before[i] = last
    for h in range(HBLK):
        last = jnp.int32(held)
        for i in range(held):
            last = jnp.where(home[i] == h, i, last)
        final[h] = last
    partial[held] = jnp.zeros_like(partial[held])

    gather_sol = [DirectGather(copies, place, shards_of(sol_all, s)) for s in range(supers)]
    store_sol = []
    gather_rhs.turn()
    gather_rhs.forward()
    gather_rhs.complete()
    loads[1].wait()
    for s in range(supers):
        sol_all[s, span(row, rows), :] = dot(dinv[s], rhs_all[s]).astype(jnp.bfloat16)
        gather_sol[s].start()
    pl.semaphore_wait(relay.at[0], 2)
    signal(relay.at[1], {"layer": layer_at(-4)})
    store_sol = pltpu.make_async_copy(
        sol_all.at[:, span(row, rows), :], sol_out.at[0], local_sem.at[11]
    )
    store_sol.start()

    near = {step: copies.take() for step in (1, -1, -2)}
    loads[2].wait()
    loads[3].wait()
    own = None
    for s in range(supers):
        gather_sol[s].forward()
        gather_sol[s].complete()
        term = dot(anc[s], sol_all[s])
        own = term if own is None else own + term
        if s == supers - 1:
            anc_own[0] = own.astype(jnp.bfloat16)
            for n, step in enumerate(near):
                copies.start(near[step], anc_own.at[0], anc_near.at[n], {"layer": layer_at(step)})
            loads[6].wait()
            gather_dinv = TreeGather(
                copies,
                place,
                lambda h, r: dinv_anc_all.at[
                    pl.ds(pl.multiple_of(r * anc_rows + h * (anc_rows // 2), anc_rows // 2), anc_rows // 2), :
                ],
                lambda r: dinv_anc_all.at[span(r, anc_rows), :],
            )
            gather_dinv.start()
        product[...] = dot(high[s], sol_all[s])
        for q in range(held // supers):
            i = s * (held // supers) + q
            partial[i] = product[q * BLOCK : (q + 1) * BLOCK, :] + partial[before[i]]

    cut = BLOCK // PIECES
    ways = (1, -1)
    far_half = {1: range(0, PIECES // 2), -1: range(PIECES // 2, PIECES)}
    chain = {(w, d, p): copies.take() for w in ways for d in (8, 6, 4, 2) for p in range(PIECES)}
    side = {(w, d): copies.take() for w in ways for d in (7, 5, 3, 1)}

    def box(w, n):
        return n if w == 1 else n + 4

    def send_chain(w, d, p, value):
        piece = pl.ds(p * cut, cut)
        at = box(w, d // 2 - 1)
        chain_out[at, piece, :] = value.astype(jnp.bfloat16)
        copies.start(
            chain[w, d, p],
            chain_out.at[at, piece, :],
            chain_in.at[at, piece, :],
            {"layer": layer_at(2 * w)},
        )

    def send_sides(d):
        for w in ways:
            at = box(w, d // 2)
            side_out[at] = partial[final[layer_at(w * d)]].astype(jnp.bfloat16)
            copies.start(side[w, d], side_out.at[at], side_in.at[at], {"layer": layer_at(w)})

    def arrived(w, d, p, value, fresh):
        piece = pl.ds(p * cut, cut)
        if d + 2 < 8 or p in far_half[w]:
            at = box(w, d // 2)
            copies.arrived(
                chain[w, d + 2, p], chain_in.at[at, piece, :], {"layer": layer_at(-2 * w)}
            )
            value = value + chain_in[at, piece, :].astype(jnp.float32)
        at = box(w, d // 2)
        if fresh:
            copies.arrived(side[w, d + 1], side_in.at[at], {"layer": layer_at(-w)})
        return value + side_in[at, piece, :].astype(jnp.float32)

    def pass_on(d):
        slots = {w: final[layer_at(w * d)] for w in ways}
        for p in range(PIECES):
            piece = pl.ds(p * cut, cut)
            for w in ways:
                value = arrived(w, d, p, partial[slots[w], piece, :], p == 0)
                send_chain(w, d, p, value)

    slot = final[layer_at(8)]
    for w in ways:
        for p in far_half[w]:
            send_chain(w, 8, p, partial[slot, pl.ds(p * cut, cut), :])
    send_sides(7)
    pl.semaphore_wait(relay.at[1], 1)
    for n, step in enumerate(near):
        copies.arrived(near[step], anc_near.at[n], {"layer": layer_at(-step)})
        own = own + anc_near[n].astype(jnp.float32)
    anc_own[1] = own.astype(jnp.bfloat16)
    far = {step: copies.take() for step in (8, 4, -4)}
    for n, step in enumerate(far):
        copies.start(far[step], anc_own.at[1], anc_far.at[n], {"layer": layer_at(step)})
    send_sides(5)
    gather_dinv.turn()
    pass_on(6)
    send_sides(3)
    gather_dinv.forward()
    pass_on(4)
    send_sides(1)
    for n, step in enumerate(far):
        copies.arrived(far[step], anc_far.at[n], {"layer": layer_at(-step)})
        own = own + anc_far[n].astype(jnp.float32)
    loads[4].wait()
    anc_all[span(row, anc_rows), :] = (rhs_anc[...] - own).astype(jnp.bfloat16)
    gather_anc = DirectGather(copies, place, lambda r: anc_all.at[span(r, anc_rows), :])
    gather_anc.start()
    gather_dinv.complete()
    loads[7].wait()
    spread = dot(lower[...], dinv_anc_all[...])
    reach[0] = spread.astype(jnp.bfloat16)
    reach[1] = (spread - reach[0].astype(jnp.float32)).astype(jnp.bfloat16)
    pass_on(2)
    gather_anc.forward()
    gather_anc.complete()
    anc_sol[...] = dot(dinv_anc_all[span(row, anc_rows), :], anc_all[...]).astype(jnp.bfloat16)
    store_anc = pltpu.make_async_copy(anc_sol, anc_out, local_sem.at[9])
    store_anc.start()
    loads[5].wait()
    result[...] = rhs_high[...] - dot(reach[0], anc_all[...]) - dot(reach[1], anc_all[...])
    slot = final[layer]
    for p in range(PIECES):
        piece = pl.ds(p * cut, cut)
        summed = partial[slot, piece, :]
        for w in ways:
            summed = arrived(w, 0, p, summed, p == 0)
        result[piece, :] = result[piece, :] - summed
    store_high = pltpu.make_async_copy(result, high_out, local_sem.at[10])
    store_high.start()
    copies.drain()
    store_sol.wait()
    store_anc.wait()
    store_high.wait()


def hand_over(*refs):
    count = len(refs) // 3
    given, wanted, held = refs[:count], refs[count : 2 * count], refs[2 * count : -1]
    sem = refs[-1]
    loads = [pltpu.make_async_copy(a, b, sem.at[0, n]) for n, (a, b) in enumerate(zip(given, held))]
    stores = [pltpu.make_async_copy(a, b, sem.at[1, n]) for n, (a, b) in enumerate(zip(held, wanted))]
    for load in loads:
        load.start()
    for load, store in zip(loads, stores):
        load.wait()
        store.start()
    for store in stores:
        store.wait()


def on_device(layers, rhs_local, dinv_local, lower_anc, lower_high, row_blocks, rhs_anc, rhs_high, dinv_anc, lower_anc_high):
    supers, rows, width = rhs_local.shape[1:]
    order = dinv_local.shape[3]
    anc_rows, anc_order = dinv_anc.shape
    held = supers * row_blocks.shape[2]
    bf16, f32 = jnp.bfloat16, jnp.float32
    anywhere = pl.BlockSpec(memory_space=pl.ANY)
    shapes = (
        jax.ShapeDtypeStruct(rhs_local.shape, bf16),
        jax.ShapeDtypeStruct(rhs_anc.shape, bf16),
        jax.ShapeDtypeStruct(rhs_high.shape, f32),
    )
    outs = pl.pallas_call(
        functools.partial(kernel, layers),
        out_shape=shapes,
        in_specs=[anywhere] * 9,
        out_specs=(anywhere,) * 3,
        scratch_shapes=[
            pltpu.VMEM(dinv_local.shape[1:], bf16),
            pltpu.VMEM(lower_anc.shape[1:], bf16),
            pltpu.VMEM(lower_high.shape[1:], bf16),
            pltpu.VMEM(rhs_anc.shape, f32),
            pltpu.VMEM(rhs_high.shape, f32),
            pltpu.VMEM((anc_order, anc_order), bf16),
            pltpu.VMEM(lower_anc_high.shape, bf16),
            pltpu.VMEM((supers, order, width), bf16),
            pltpu.VMEM((supers, order, width), bf16),
            pltpu.VMEM((anc_order, width), bf16),
            pltpu.VMEM((anc_rows, width), bf16),
            pltpu.VMEM((held + 1, BLOCK, width), f32),
            pltpu.VMEM((lower_high.shape[2], width), f32),
            pltpu.VMEM((2, BLOCK, anc_order), bf16),
            pltpu.VMEM((8, BLOCK, width), bf16),
            pltpu.VMEM((8, BLOCK, width), bf16),
            pltpu.VMEM((8, BLOCK, width), bf16),
            pltpu.VMEM((8, BLOCK, width), bf16),
            pltpu.VMEM((3, anc_rows, width), bf16),
            pltpu.VMEM((3, anc_rows, width), bf16),
            pltpu.VMEM((2, anc_rows, width), bf16),
            pltpu.VMEM(rhs_high.shape, f32),
            pltpu.SMEM(row_blocks.shape, jnp.int32),
            pltpu.SMEM((held,), jnp.int32),
            pltpu.SMEM((HBLK,), jnp.int32),
            pltpu.SemaphoreType.DMA((256,)),
            pltpu.SemaphoreType.DMA((256,)),
            pltpu.SemaphoreType.DMA((12,)),
            pltpu.SemaphoreType.REGULAR((2,)),
        ],
        compiler_params=pltpu.CompilerParams(collective_id=0, has_side_effects=True),
    )(row_blocks, rhs_local, dinv_local, lower_anc, lower_high, rhs_anc, rhs_high, dinv_anc, lower_anc_high)
    return pl.pallas_call(
        hand_over,
        out_shape=shapes,
        in_specs=[anywhere] * 3,
        out_specs=(anywhere,) * 3,
        scratch_shapes=[pltpu.VMEM(a.shape, a.dtype) for a in shapes]
        + [pltpu.SemaphoreType.DMA((2, 3))],
    )(*outs)


def solution(mesh):
    return jax.shard_map(
        functools.partial(on_device, mesh.shape["layer"]),
        mesh=mesh,
        in_specs=(
            P("layer", None, "row", None),
            P("layer", None, "row", None),
            P("layer", None, "row", None),
            P("layer", None, "row", None),
            P("layer", None, "row"),
            P("row", None),
            P(("row", "layer"), None),
            P("row", None),
            P(("row", "layer"), None),
        ),
        out_specs=(P("layer", None, "row", None), P("row", None), P(("row", "layer"), None)),
        check_vma=False,
    )
```

```python
import functools

import jax
import jax.numpy as jnp
from jax import lax
from jax.experimental import pallas as pl
from jax.experimental.pallas import tpu as pltpu
from jax.sharding import PartitionSpec as P

BLOCK = 128
HBLK = 16
X, Y, CORES = 4, 4, 2
PIECES = 4


class Copies:
    def __init__(self, send_sem, recv_sem):
        self.send_sem, self.recv_sem = send_sem, recv_sem
        self.used = 0
        self.started = []

    def take(self, count=1):
        first = self.used
        self.used += count
        return first

    def start(self, index, src, dst, device):
        copy = pltpu.make_async_remote_copy(
            src_ref=src,
            dst_ref=dst,
            send_sem=self.send_sem.at[index],
            recv_sem=self.recv_sem.at[index],
            device_id=device,
            device_id_type=pl.DeviceIdType.MESH,
        )
        copy.start()
        self.started.append(copy)

    def arrived(self, index, dst, device):
        pltpu.make_async_remote_copy(
            src_ref=dst,
            dst_ref=dst,
            send_sem=self.send_sem.at[index],
            recv_sem=self.recv_sem.at[index],
            device_id=device,
            device_id_type=pl.DeviceIdType.MESH,
        ).wait_recv()

    def drain(self, count=None):
        count = len(self.started) if count is None else count
        for copy in self.started[:count]:
            copy.wait_send()
        self.started = self.started[count:]


class Place:
    def __init__(self):
        row = lax.axis_index("row")
        self.row = row
        self.x = row // (Y * CORES)
        self.y = (row // CORES) % Y
        self.core = row % CORES

    def at(self, dx, dy, flip=False):
        x = lax.rem(self.x + (dx + X), X)
        y = lax.rem(self.y + (dy + Y), Y)
        core = 1 - self.core if flip else self.core
        return (x * Y + y) * CORES + core


class TreeGather:
    def __init__(self, copies, place, half, both):
        self.copies, self.place, self.half, self.both = copies, place, half, both
        self.order = [(dx, dy) for dx in range(X) for dy in range(Y) if dx or dy]
        self.order.sort(key=lambda p: (min(p[0], X - p[0]) + min(p[1], Y - p[1]), p))
        self.first = {(h, d): copies.take() for h in (0, 1) for d in (1, 2, 3)}
        self.second = {
            (h, e, d): copies.take() for h in (0, 1) for e in range(4) for d in (1, 2, 3)
        }
        self.other = {(dx, dy): copies.take() for dx in range(X) for dy in range(Y)}

    def along(self, h, d, e):
        return (d, e) if h == 0 else (e, d)

    def send_first(self, h, d):
        at = self.place.at
        shard = self.half(h, at(0, 0))
        self.copies.start(self.first[h, d], shard, shard, {"row": at(*self.along(h, d, 0))})

    def send_second(self, h, e):
        at = self.place.at
        shard = self.half(h, at(*self.along(h, -e, 0)))
        for d in (1, 3, 2):
            self.copies.start(
                self.second[h, e, d], shard, shard, {"row": at(*self.along(h, 0, d))}
            )

    def send_other(self, dx, dy):
        at = self.place.at
        shard = self.both(at(-dx, -dy))
        self.copies.start(self.other[dx, dy], shard, shard, {"row": at(0, 0, True)})

    def start(self):
        for d in (1, 3, 2):
            for h in (0, 1):
                self.send_first(h, d)
        for h in (0, 1):
            self.send_second(h, 0)
        self.send_other(0, 0)

    def turn(self):
        at = self.place.at
        for e in (1, 3, 2):
            for h in (0, 1):
                self.copies.arrived(
                    self.first[h, e],
                    self.half(h, at(*self.along(h, -e, 0))),
                    {"row": at(*self.along(h, -e, 0))},
                )
                self.send_second(h, e)

    def forward(self):
        at = self.place.at
        for dx, dy in self.order:
            source = at(-dx, -dy)
            if dy:
                self.copies.arrived(
                    self.second[0, dx, dy], self.half(0, source), {"row": at(0, -dy)}
                )
            if dx:
                self.copies.arrived(
                    self.second[1, dy, dx], self.half(1, source), {"row": at(-dx, 0)}
                )
            self.send_other(dx, dy)

    def complete(self):
        at = self.place.at
        for dx, dy in [(0, 0)] + self.order:
            self.copies.arrived(
                self.other[dx, dy], self.both(at(-dx, -dy, True)), {"row": at(0, 0, True)}
            )


class DirectGather:
    def __init__(self, copies, place, shard):
        self.copies, self.place, self.shard = copies, place, shard
        self.order = [(dx, dy) for dx in range(X) for dy in range(Y) if dx or dy]
        self.order.sort(key=lambda p: (min(p[0], X - p[0]) + min(p[1], Y - p[1]), p))
        self.peer = {p: copies.take() for p in self.order}
        self.other = {p: copies.take() for p in [(0, 0)] + self.order}

    def start(self):
        at = self.place.at
        mine = self.shard(at(0, 0))
        for p in reversed(self.order):
            self.copies.start(self.peer[p], mine, mine, {"row": at(*p)})
        self.send_other(0, 0)

    def send_other(self, dx, dy):
        at = self.place.at
        shard = self.shard(at(-dx, -dy))
        self.copies.start(self.other[dx, dy], shard, shard, {"row": at(0, 0, True)})

    def forward(self):
        at = self.place.at
        for dx, dy in self.order:
            self.copies.arrived(
                self.peer[dx, dy], self.shard(at(-dx, -dy)), {"row": at(-dx, -dy)}
            )
            self.send_other(dx, dy)

    def complete(self):
        at = self.place.at
        for dx, dy in [(0, 0)] + self.order:
            self.copies.arrived(
                self.other[dx, dy], self.shard(at(-dx, -dy, True)), {"row": at(0, 0, True)}
            )


def dot(a, b):
    return jnp.dot(a, b, preferred_element_type=jnp.float32)


def kernel(
    layers,
    blocks_hbm,
    rhs_hbm,
    dinv_hbm,
    anc_hbm,
    high_hbm,
    rhs_anc_hbm,
    rhs_high_hbm,
    dinv_anc_hbm,
    lower_hbm,
    sol_out,
    anc_out,
    high_out,
    dinv,
    anc,
    high,
    rhs_anc,
    rhs_high,
    dinv_anc_all,
    lower,
    rhs_all,
    sol_all,
    anc_all,
    partial,
    product,
    reach,
    chain_in,
    chain_out,
    side_in,
    side_out,
    anc_near,
    anc_far,
    anc_own,
    blocks_ref,
    before,
    final,
    send_sem,
    recv_sem,
    local_sem,
    relay,
):
    place = Place()
    row = place.row
    layer = lax.axis_index("layer")
    copies = Copies(send_sem, recv_sem)
    supers, rows, width = sol_out.shape[1:]
    held = supers * blocks_ref.shape[2]
    anc_rows = rhs_anc.shape[0]

    def layer_at(step):
        return lax.rem(layer + (step + layers), layers)

    def signal(sem, where):
        pl.semaphore_signal(sem, inc=1, device_id=where, device_id_type=pl.DeviceIdType.MESH)

    def span(r, count):
        return pl.ds(pl.multiple_of(r * count, count), count)

    def shards_of(ref, s):
        return lambda r: ref.at[s, span(r, rows), :]

    barrier = pltpu.get_barrier_semaphore()
    lines = [(d, 0) for d in (2, 1, 3)] + [(0, d) for d in (2, 1, 3)]
    along = [1, -1, 2, -2]
    for step in along:
        signal(barrier, {"layer": layer_at(step)})
    for dx, dy in lines:
        signal(barrier, {"row": place.at(dx, dy)})
    signal(barrier, {"row": place.at(0, 0, True)})

    loads = []
    for n, (src, dst) in enumerate(
        (
            (rhs_hbm.at[0], rhs_all.at[:, span(row, rows), :]),
            (dinv_hbm.at[0], dinv),
            (anc_hbm.at[0], anc),
            (high_hbm.at[0], high),
            (rhs_anc_hbm, rhs_anc),
            (rhs_high_hbm, rhs_high),
            (dinv_anc_hbm, dinv_anc_all.at[span(row, anc_rows), :]),
            (lower_hbm, lower),
            (blocks_hbm, blocks_ref),
        )
    ):
        load = pltpu.make_async_copy(src, dst, local_sem.at[n])
        load.start()
        loads.append(load)

    loads[0].wait()
    pl.semaphore_wait(barrier, len(lines) + 1 + len(along))
    for step in (2, -2):
        signal(relay.at[0], {"layer": layer_at(step)})

    gather_rhs = TreeGather(
        copies,
        place,
        lambda h, r: rhs_all.at[h, span(r, rows), :],
        lambda r: rhs_all.at[:, span(r, rows), :],
    )
    gather_rhs.start()
    loads[8].wait()
    home = [blocks_ref[0, i // (held // supers), i % (held // supers)] for i in range(held)]
    for i in range(held):
        last = jnp.int32(held)
        for j in range(i):
            last = jnp.where(home[j] == home[i], j, last)
        before[i] = last
    for h in range(HBLK):
        last = jnp.int32(held)
        for i in range(held):
            last = jnp.where(home[i] == h, i, last)
        final[h] = last
    partial[held] = jnp.zeros_like(partial[held])

    gather_sol = [DirectGather(copies, place, shards_of(sol_all, s)) for s in range(supers)]
    store_sol = []
    gather_rhs.turn()
    gather_rhs.forward()
    gather_rhs.complete()
    loads[1].wait()
    for s in range(supers):
        sol_all[s, span(row, rows), :] = dot(dinv[s], rhs_all[s]).astype(jnp.bfloat16)
        gather_sol[s].start()
    pl.semaphore_wait(relay.at[0], 2)
    signal(relay.at[1], {"layer": layer_at(-4)})
    sol_out[0] = sol_all[:, span(row, rows), :]

    near = {step: copies.take() for step in (1, -1, -2)}
    loads[2].wait()
    loads[3].wait()
    own = None
    for s in range(supers):
        gather_sol[s].forward()
        gather_sol[s].complete()
        term = dot(anc[s], sol_all[s])
        own = term if own is None else own + term
        if s == supers - 1:
            anc_own[0] = own.astype(jnp.bfloat16)
            for n, step in enumerate(near):
                copies.start(near[step], anc_own.at[0], anc_near.at[n], {"layer": layer_at(step)})
            loads[6].wait()
            gather_dinv = TreeGather(
                copies,
                place,
                lambda h, r: dinv_anc_all.at[
                    pl.ds(pl.multiple_of(r * anc_rows + h * (anc_rows // 2), anc_rows // 2), anc_rows // 2), :
                ],
                lambda r: dinv_anc_all.at[span(r, anc_rows), :],
            )
            gather_dinv.start()
        product[...] = dot(high[s], sol_all[s])
        for q in range(held // supers):
            i = s * (held // supers) + q
            partial[i] = product[q * BLOCK : (q + 1) * BLOCK, :] + partial[before[i]]

    cut = BLOCK // PIECES
    ways = (1, -1)
    far_half = {1: range(0, PIECES // 2), -1: range(PIECES // 2, PIECES)}
    chain = {(w, d, p): copies.take() for w in ways for d in (8, 6, 4, 2) for p in range(PIECES)}
    side = {(w, d): copies.take() for w in ways for d in (7, 5, 3, 1)}

    def box(w, n):
        return n if w == 1 else n + 4

    def send_chain(w, d, p, value):
        piece = pl.ds(p * cut, cut)
        at = box(w, d // 2 - 1)
        chain_out[at, piece, :] = value.astype(jnp.bfloat16)
        copies.start(
            chain[w, d, p],
            chain_out.at[at, piece, :],
            chain_in.at[at, piece, :],
            {"layer": layer_at(2 * w)},
        )

    def send_sides(d):
        for w in ways:
            at = box(w, d // 2)
            side_out[at] = partial[final[layer_at(w * d)]].astype(jnp.bfloat16)
            copies.start(side[w, d], side_out.at[at], side_in.at[at], {"layer": layer_at(w)})

    def arrived(w, d, p, value, fresh):
        piece = pl.ds(p * cut, cut)
        if d + 2 < 8 or p in far_half[w]:
            at = box(w, d // 2)
            copies.arrived(
                chain[w, d + 2, p], chain_in.at[at, piece, :], {"layer": layer_at(-2 * w)}
            )
            value = value + chain_in[at, piece, :].astype(jnp.float32)
        at = box(w, d // 2)
        if fresh:
            copies.arrived(side[w, d + 1], side_in.at[at], {"layer": layer_at(-w)})
        return value + side_in[at, piece, :].astype(jnp.float32)

    def pass_on(d):
        slots = {w: final[layer_at(w * d)] for w in ways}
        for p in range(PIECES):
            piece = pl.ds(p * cut, cut)
            for w in ways:
                value = arrived(w, d, p, partial[slots[w], piece, :], p == 0)
                send_chain(w, d, p, value)

    slot = final[layer_at(8)]
    for w in ways:
        for p in far_half[w]:
            send_chain(w, 8, p, partial[slot, pl.ds(p * cut, cut), :])
    send_sides(7)
    pl.semaphore_wait(relay.at[1], 1)
    for n, step in enumerate(near):
        copies.arrived(near[step], anc_near.at[n], {"layer": layer_at(-step)})
        own = own + anc_near[n].astype(jnp.float32)
    anc_own[1] = own.astype(jnp.bfloat16)
    far = {step: copies.take() for step in (8, 4, -4)}
    for n, step in enumerate(far):
        copies.start(far[step], anc_own.at[1], anc_far.at[n], {"layer": layer_at(step)})
    send_sides(5)
    gather_dinv.turn()
    pass_on(6)
    send_sides(3)
    gather_dinv.forward()
    sent = len(copies.started)
    pass_on(4)
    send_sides(1)
    copies.drain(sent)
    for n, step in enumerate(far):
        copies.arrived(far[step], anc_far.at[n], {"layer": layer_at(-step)})
        own = own + anc_far[n].astype(jnp.float32)
    loads[4].wait()
    anc_all[span(row, anc_rows), :] = (rhs_anc[...] - own).astype(jnp.bfloat16)
    gather_anc = DirectGather(copies, place, lambda r: anc_all.at[span(r, anc_rows), :])
    gather_anc.start()
    gather_dinv.complete()
    loads[7].wait()
    spread = dot(lower[...], dinv_anc_all[...])
    reach[0] = spread.astype(jnp.bfloat16)
    reach[1] = (spread - reach[0].astype(jnp.float32)).astype(jnp.bfloat16)
    pass_on(2)
    gather_anc.forward()
    gather_anc.complete()
    loads[5].wait()
    high_out[...] = rhs_high[...] - dot(reach[0], anc_all[...]) - dot(reach[1], anc_all[...])
    slot = final[layer]
    for p in range(PIECES):
        piece = pl.ds(p * cut, cut)
        summed = partial[slot, piece, :]
        for w in ways:
            summed = arrived(w, 0, p, summed, p == 0)
        high_out[piece, :] = high_out[piece, :] - summed
    anc_out[...] = dot(dinv_anc_all[span(row, anc_rows), :], anc_all[...]).astype(jnp.bfloat16)
    copies.drain()


def hand_over(*refs):
    count = len(refs) // 2
    stores = [
        pltpu.make_async_copy(refs[n], refs[count + n], refs[-1].at[n]) for n in range(count)
    ]
    for store in stores:
        store.start()
    for store in stores:
        store.wait()


def on_device(layers, rhs_local, dinv_local, lower_anc, lower_high, row_blocks, rhs_anc, rhs_high, dinv_anc, lower_anc_high):
    supers, rows, width = rhs_local.shape[1:]
    order = dinv_local.shape[3]
    anc_rows, anc_order = dinv_anc.shape
    held = supers * row_blocks.shape[2]
    bf16, f32 = jnp.bfloat16, jnp.float32
    anywhere = pl.BlockSpec(memory_space=pl.ANY)
    shapes = (
        jax.ShapeDtypeStruct(rhs_local.shape, bf16),
        jax.ShapeDtypeStruct(rhs_anc.shape, bf16),
        jax.ShapeDtypeStruct(rhs_high.shape, f32),
    )
    outs = pl.pallas_call(
        functools.partial(kernel, layers),
        out_shape=shapes,
        in_specs=[anywhere] * 9,
        out_specs=(pl.BlockSpec(memory_space=pltpu.VMEM),) * 3,
        scratch_shapes=[
            pltpu.VMEM(dinv_local.shape[1:], bf16),
            pltpu.VMEM(lower_anc.shape[1:], bf16),
            pltpu.VMEM(lower_high.shape[1:], bf16),
            pltpu.VMEM(rhs_anc.shape, f32),
            pltpu.VMEM(rhs_high.shape, f32),
            pltpu.VMEM((anc_order, anc_order), bf16),
            pltpu.VMEM(lower_anc_high.shape, bf16),
            pltpu.VMEM((supers, order, width), bf16),
            pltpu.VMEM((supers, order, width), bf16),
            pltpu.VMEM((anc_order, width), bf16),
            pltpu.VMEM((held + 1, BLOCK, width), f32),
            pltpu.VMEM((lower_high.shape[2], width), f32),
            pltpu.VMEM((2, BLOCK, anc_order), bf16),
            pltpu.VMEM((8, BLOCK, width), bf16),
            pltpu.VMEM((8, BLOCK, width), bf16),
            pltpu.VMEM((8, BLOCK, width), bf16),
            pltpu.VMEM((8, BLOCK, width), bf16),
            pltpu.VMEM((3, anc_rows, width), bf16),
            pltpu.VMEM((3, anc_rows, width), bf16),
            pltpu.VMEM((2, anc_rows, width), bf16),
            pltpu.SMEM(row_blocks.shape, jnp.int32),
            pltpu.SMEM((held,), jnp.int32),
            pltpu.SMEM((HBLK,), jnp.int32),
            pltpu.SemaphoreType.DMA((256,)),
            pltpu.SemaphoreType.DMA((256,)),
            pltpu.SemaphoreType.DMA((12,)),
            pltpu.SemaphoreType.REGULAR((2,)),
        ],
        compiler_params=pltpu.CompilerParams(collective_id=0, has_side_effects=True, vmem_limit_bytes=24 << 20),
    )(*[pltpu.with_memory_space_constraint(a, pltpu.HBM) for a in (row_blocks, rhs_local, dinv_local, lower_anc, lower_high, rhs_anc, rhs_high, dinv_anc, lower_anc_high)])
    return pl.pallas_call(
        hand_over,
        out_shape=shapes,
        in_specs=[pl.BlockSpec(memory_space=pltpu.VMEM)] * 3,
        out_specs=(anywhere,) * 3,
        scratch_shapes=[pltpu.SemaphoreType.DMA((3,))],
        compiler_params=pltpu.CompilerParams(vmem_limit_bytes=4 << 20),
    )(*outs)


def solution(mesh):
    return jax.shard_map(
        functools.partial(on_device, mesh.shape["layer"]),
        mesh=mesh,
        in_specs=(
            P("layer", None, "row", None),
            P("layer", None, "row", None),
            P("layer", None, "row", None),
            P("layer", None, "row", None),
            P("layer", None, "row"),
            P("row", None),
            P(("row", "layer"), None),
            P("row", None),
            P(("row", "layer"), None),
        ),
        out_specs=(P("layer", None, "row", None), P("row", None), P(("row", "layer"), None)),
        check_vma=False,
    )
```

```python
import functools

import jax
import jax.numpy as jnp
from jax import lax
from jax.experimental import pallas as pl
from jax.experimental.pallas import tpu as pltpu
from jax.sharding import PartitionSpec as P

BLOCK = 128
HBLK = 16
X, Y, CORES = 4, 4, 2
PIECES = 4


class Copies:
    def __init__(self, send_sem, recv_sem):
        self.send_sem, self.recv_sem = send_sem, recv_sem
        self.used = 0
        self.started = []

    def take(self, count=1):
        first = self.used
        self.used += count
        return first

    def start(self, index, src, dst, device):
        copy = pltpu.make_async_remote_copy(
            src_ref=src,
            dst_ref=dst,
            send_sem=self.send_sem.at[index],
            recv_sem=self.recv_sem.at[index],
            device_id=device,
            device_id_type=pl.DeviceIdType.MESH,
        )
        copy.start()
        self.started.append(copy)

    def arrived(self, index, dst, device):
        pltpu.make_async_remote_copy(
            src_ref=dst,
            dst_ref=dst,
            send_sem=self.send_sem.at[index],
            recv_sem=self.recv_sem.at[index],
            device_id=device,
            device_id_type=pl.DeviceIdType.MESH,
        ).wait_recv()

    def drain(self, count=None):
        count = len(self.started) if count is None else count
        for copy in self.started[:count]:
            copy.wait_send()
        self.started = self.started[count:]


class Place:
    def __init__(self):
        row = lax.axis_index("row")
        self.row = row
        self.x = row // (Y * CORES)
        self.y = (row // CORES) % Y
        self.core = row % CORES
        self.known = {}

    def at(self, dx, dy, flip=False):
        key = dx % X, dy % Y, flip
        if key not in self.known:
            self.known[key] = self.find(*key)
        return self.known[key]

    def find(self, dx, dy, flip):
        x = lax.rem(self.x + (dx + X), X)
        y = lax.rem(self.y + (dy + Y), Y)
        core = 1 - self.core if flip else self.core
        return (x * Y + y) * CORES + core


class TreeGather:
    def __init__(self, copies, place, half, both):
        self.copies, self.place, self.half, self.both = copies, place, half, both
        self.order = [(dx, dy) for dx in range(X) for dy in range(Y) if dx or dy]
        self.order.sort(key=lambda p: (min(p[0], X - p[0]) + min(p[1], Y - p[1]), p))
        self.first = {(h, d): copies.take() for h in (0, 1) for d in (1, 2, 3)}
        self.second = {
            (h, e, d): copies.take() for h in (0, 1) for e in range(4) for d in (1, 2, 3)
        }
        self.other = {(dx, dy): copies.take() for dx in range(X) for dy in range(Y)}

    def along(self, h, d, e):
        return (d, e) if h == 0 else (e, d)

    def send_first(self, h, d):
        at = self.place.at
        shard = self.half(h, at(0, 0))
        self.copies.start(self.first[h, d], shard, shard, {"row": at(*self.along(h, d, 0))})

    def send_second(self, h, e):
        at = self.place.at
        shard = self.half(h, at(*self.along(h, -e, 0)))
        for d in (1, 3, 2):
            self.copies.start(
                self.second[h, e, d], shard, shard, {"row": at(*self.along(h, 0, d))}
            )

    def send_other(self, dx, dy):
        at = self.place.at
        shard = self.both(at(-dx, -dy))
        self.copies.start(self.other[dx, dy], shard, shard, {"row": at(0, 0, True)})

    def start(self):
        for d in (1, 3, 2):
            for h in (0, 1):
                self.send_first(h, d)
        for h in (0, 1):
            self.send_second(h, 0)
        self.send_other(0, 0)

    def turn(self):
        at = self.place.at
        for e in (1, 3, 2):
            for h in (0, 1):
                self.copies.arrived(
                    self.first[h, e],
                    self.half(h, at(*self.along(h, -e, 0))),
                    {"row": at(*self.along(h, -e, 0))},
                )
                self.send_second(h, e)

    def forward(self):
        at = self.place.at
        for dx, dy in self.order:
            source = at(-dx, -dy)
            if dy:
                self.copies.arrived(
                    self.second[0, dx, dy], self.half(0, source), {"row": at(0, -dy)}
                )
            if dx:
                self.copies.arrived(
                    self.second[1, dy, dx], self.half(1, source), {"row": at(-dx, 0)}
                )
            self.send_other(dx, dy)

    def complete(self):
        at = self.place.at
        for dx, dy in [(0, 0)] + self.order:
            self.copies.arrived(
                self.other[dx, dy], self.both(at(-dx, -dy, True)), {"row": at(0, 0, True)}
            )


class DirectGather:
    def __init__(self, copies, place, shard):
        self.copies, self.place, self.shard = copies, place, shard
        self.order = [(dx, dy) for dx in range(X) for dy in range(Y) if dx or dy]
        self.order.sort(key=lambda p: (min(p[0], X - p[0]) + min(p[1], Y - p[1]), p))
        self.peer = {p: copies.take() for p in self.order}
        self.other = {p: copies.take() for p in [(0, 0)] + self.order}

    def start(self):
        at = self.place.at
        mine = self.shard(at(0, 0))
        for p in reversed(self.order):
            self.copies.start(self.peer[p], mine, mine, {"row": at(*p)})
        self.send_other(0, 0)

    def send_other(self, dx, dy):
        at = self.place.at
        shard = self.shard(at(-dx, -dy))
        self.copies.start(self.other[dx, dy], shard, shard, {"row": at(0, 0, True)})

    def forward(self):
        at = self.place.at
        for dx, dy in self.order:
            self.copies.arrived(
                self.peer[dx, dy], self.shard(at(-dx, -dy)), {"row": at(-dx, -dy)}
            )
            self.send_other(dx, dy)

    def complete(self):
        at = self.place.at
        for dx, dy in [(0, 0)] + self.order:
            self.copies.arrived(
                self.other[dx, dy], self.shard(at(-dx, -dy, True)), {"row": at(0, 0, True)}
            )


class BulkGather(TreeGather):
    def __init__(self, copies, place, half, both, all_of):
        super().__init__(copies, place, half, both)
        self.all_of = all_of
        self.bulk = self.other[self.order[-1]]

    def send_other(self, dx, dy):
        if (dx, dy) == self.order[-1]:
            mine = self.all_of(self.place.core)
            self.copies.start(self.bulk, mine, mine, {"row": self.place.at(0, 0, True)})

    def complete(self):
        self.copies.arrived(
            self.bulk, self.all_of(1 - self.place.core), {"row": self.place.at(0, 0, True)}
        )


def dot(a, b):
    return jnp.dot(a, b, preferred_element_type=jnp.float32)


def kernel(
    layers,
    blocks_hbm,
    rhs_hbm,
    dinv_hbm,
    anc_hbm,
    high_hbm,
    rhs_anc_hbm,
    rhs_high_hbm,
    dinv_anc_hbm,
    lower_hbm,
    sol_out,
    anc_out,
    high_out,
    dinv,
    anc,
    high,
    rhs_anc,
    rhs_high,
    dinv_anc_all,
    lower,
    rhs_all,
    sol_all,
    anc_all,
    partial,
    product,
    reach,
    chain_in,
    chain_out,
    side_in,
    side_out,
    anc_near,
    anc_far,
    anc_own,
    blocks_ref,
    before,
    final,
    send_sem,
    recv_sem,
    local_sem,
    relay,
):
    place = Place()
    row = place.row
    layer = lax.axis_index("layer")
    copies = Copies(send_sem, recv_sem)
    supers, rows, width = sol_out.shape[1:]
    held = supers * blocks_ref.shape[2]
    anc_rows = rhs_anc.shape[0]

    others = {}

    def layer_at(step):
        key = step % layers
        if key not in others:
            others[key] = lax.rem(layer + key, layers)
        return others[key]

    def signal(sem, where):
        pl.semaphore_signal(sem, inc=1, device_id=where, device_id_type=pl.DeviceIdType.MESH)

    def span(r, count):
        return pl.ds(pl.multiple_of(r * count, count), count)

    def shards_of(ref, s):
        return lambda r: ref.at[s, span(r, rows), :]

    barrier = pltpu.get_barrier_semaphore()
    lines = [(d, 0) for d in (2, 1, 3)] + [(0, d) for d in (2, 1, 3)]
    along = [1, -1, 2, -2]
    for step in along:
        signal(barrier, {"layer": layer_at(step)})
    for dx, dy in lines:
        signal(barrier, {"row": place.at(dx, dy)})
    signal(barrier, {"row": place.at(0, 0, True)})

    loads = []
    for n, (src, dst) in enumerate(
        (
            (rhs_hbm.at[0], rhs_all.at[:, span(row, rows), :]),
            (dinv_hbm.at[0], dinv),
            (anc_hbm.at[0], anc),
            (high_hbm.at[0], high),
            (rhs_anc_hbm, rhs_anc),
            (rhs_high_hbm, rhs_high),
            (dinv_anc_hbm, dinv_anc_all.at[row // CORES, row % CORES]),
            (lower_hbm, lower),
            (blocks_hbm, blocks_ref),
        )
    ):
        load = pltpu.make_async_copy(src, dst, local_sem.at[n])
        load.start()
        loads.append(load)

    loads[0].wait()
    pl.semaphore_wait(barrier, len(lines) + 1 + len(along))
    for step in (2, -2):
        signal(relay.at[0], {"layer": layer_at(step)})

    gather_rhs = TreeGather(
        copies,
        place,
        lambda h, r: rhs_all.at[h, span(r, rows), :],
        lambda r: rhs_all.at[:, span(r, rows), :],
    )
    gather_rhs.start()
    loads[8].wait()
    home = [blocks_ref[0, i // (held // supers), i % (held // supers)] for i in range(held)]
    for i in range(held):
        last = jnp.int32(held)
        for j in range(i):
            last = jnp.where(home[j] == home[i], j, last)
        before[i] = last
    for h in range(HBLK):
        last = jnp.int32(held)
        for i in range(held):
            last = jnp.where(home[i] == h, i, last)
        final[h] = last
    partial[held] = jnp.zeros_like(partial[held])

    gather_sol = [DirectGather(copies, place, shards_of(sol_all, s)) for s in range(supers)]
    store_sol = []
    gather_rhs.turn()
    gather_rhs.forward()
    gather_rhs.complete()
    loads[1].wait()
    for s in range(supers):
        sol_all[s, span(row, rows), :] = dot(dinv[s], rhs_all[s]).astype(jnp.bfloat16)
        gather_sol[s].start()
    pl.semaphore_wait(relay.at[0], 2)
    signal(relay.at[1], {"layer": layer_at(-4)})
    sol_out[0] = sol_all[:, span(row, rows), :]

    near = {step: copies.take() for step in (1, -1, -2)}
    loads[2].wait()
    loads[3].wait()
    own = None
    for s in range(supers):
        gather_sol[s].forward()
        gather_sol[s].complete()
        term = dot(anc[s], sol_all[s])
        own = term if own is None else own + term
        if s == supers - 1:
            anc_own[0] = own.astype(jnp.bfloat16)
            for n, step in enumerate(near):
                copies.start(near[step], anc_own.at[0], anc_near.at[n], {"layer": layer_at(step)})
            loads[6].wait()
            gather_dinv = BulkGather(
                copies,
                place,
                lambda h, r: dinv_anc_all.at[
                    r // CORES, r % CORES, pl.ds(h * (anc_rows // 2), anc_rows // 2), :
                ],
                lambda r: dinv_anc_all.at[r // CORES, r % CORES],
                lambda core: dinv_anc_all.at[:, core],
            )
            gather_dinv.start()
        product[...] = dot(high[s], sol_all[s])
        for q in range(held // supers):
            i = s * (held // supers) + q
            partial[i] = product[q * BLOCK : (q + 1) * BLOCK, :] + partial[before[i]]

    cut = BLOCK // PIECES
    ways = (1, -1)
    far_half = {1: range(0, PIECES // 2), -1: range(PIECES // 2, PIECES)}
    chain = {(w, d, p): copies.take() for w in ways for d in (8, 6, 4, 2) for p in range(PIECES)}
    side = {(w, d): copies.take() for w in ways for d in (7, 5, 3, 1)}

    def box(w, n):
        return n if w == 1 else n + 4

    def send_chain(w, d, p, value):
        piece = pl.ds(p * cut, cut)
        at = box(w, d // 2 - 1)
        chain_out[at, piece, :] = value.astype(jnp.bfloat16)
        copies.start(
            chain[w, d, p],
            chain_out.at[at, piece, :],
            chain_in.at[at, piece, :],
            {"layer": layer_at(2 * w)},
        )

    def send_sides(d):
        for w in ways:
            at = box(w, d // 2)
            side_out[at] = partial[final[layer_at(w * d)]].astype(jnp.bfloat16)
            copies.start(side[w, d], side_out.at[at], side_in.at[at], {"layer": layer_at(w)})

    def arrived(w, d, p, value, fresh):
        piece = pl.ds(p * cut, cut)
        if d + 2 < 8 or p in far_half[w]:
            at = box(w, d // 2)
            copies.arrived(
                chain[w, d + 2, p], chain_in.at[at, piece, :], {"layer": layer_at(-2 * w)}
            )
            value = value + chain_in[at, piece, :].astype(jnp.float32)
        at = box(w, d // 2)
        if fresh:
            copies.arrived(side[w, d + 1], side_in.at[at], {"layer": layer_at(-w)})
        return value + side_in[at, piece, :].astype(jnp.float32)

    def pass_on(d):
        slots = {w: final[layer_at(w * d)] for w in ways}
        for p in range(PIECES):
            piece = pl.ds(p * cut, cut)
            for w in ways:
                value = arrived(w, d, p, partial[slots[w], piece, :], p == 0)
                send_chain(w, d, p, value)

    slot = final[layer_at(8)]
    for w in ways:
        for p in far_half[w]:
            send_chain(w, 8, p, partial[slot, pl.ds(p * cut, cut), :])
    send_sides(7)
    pl.semaphore_wait(relay.at[1], 1)
    for n, step in enumerate(near):
        copies.arrived(near[step], anc_near.at[n], {"layer": layer_at(-step)})
        own = own + anc_near[n].astype(jnp.float32)
    anc_own[1] = own.astype(jnp.bfloat16)
    far = {step: copies.take() for step in (8, 4, -4)}
    for n, step in enumerate(far):
        copies.start(far[step], anc_own.at[1], anc_far.at[n], {"layer": layer_at(step)})
    send_sides(5)
    gather_dinv.turn()
    pass_on(6)
    send_sides(3)
    sent = len(copies.started)
    pass_on(4)
    send_sides(1)
    gather_dinv.forward()
    copies.drain(sent)
    for n, step in enumerate(far):
        copies.arrived(far[step], anc_far.at[n], {"layer": layer_at(-step)})
        own = own + anc_far[n].astype(jnp.float32)
    loads[4].wait()
    anc_all[span(row, anc_rows), :] = (rhs_anc[...] - own).astype(jnp.bfloat16)
    gather_anc = DirectGather(copies, place, lambda r: anc_all.at[span(r, anc_rows), :])
    gather_anc.start()
    pass_on(2)
    gather_dinv.complete()
    loads[7].wait()
    spread = dot(lower[...], dinv_anc_all[...].reshape(lower.shape[1], lower.shape[1]))
    reach[0] = spread.astype(jnp.bfloat16)
    reach[1] = (spread - reach[0].astype(jnp.float32)).astype(jnp.bfloat16)
    gather_anc.forward()
    gather_anc.complete()
    loads[5].wait()
    high_out[...] = rhs_high[...] - dot(reach[0], anc_all[...]) - dot(reach[1], anc_all[...])
    slot = final[layer]
    for p in range(PIECES):
        piece = pl.ds(p * cut, cut)
        summed = partial[slot, piece, :]
        for w in ways:
            summed = arrived(w, 0, p, summed, p == 0)
        high_out[piece, :] = high_out[piece, :] - summed
    anc_out[...] = dot(dinv_anc_all[row // CORES, row % CORES], anc_all[...]).astype(jnp.bfloat16)
    copies.drain()


def hand_over(*refs):
    count = len(refs) // 2
    stores = [
        pltpu.make_async_copy(refs[n], refs[count + n], refs[-1].at[n]) for n in range(count)
    ]
    for store in stores:
        store.start()
    for store in stores:
        store.wait()


def on_device(layers, rhs_local, dinv_local, lower_anc, lower_high, row_blocks, rhs_anc, rhs_high, dinv_anc, lower_anc_high):
    supers, rows, width = rhs_local.shape[1:]
    order = dinv_local.shape[3]
    anc_rows, anc_order = dinv_anc.shape
    held = supers * row_blocks.shape[2]
    bf16, f32 = jnp.bfloat16, jnp.float32
    anywhere = pl.BlockSpec(memory_space=pl.ANY)
    shapes = (
        jax.ShapeDtypeStruct(rhs_local.shape, bf16),
        jax.ShapeDtypeStruct(rhs_anc.shape, bf16),
        jax.ShapeDtypeStruct(rhs_high.shape, f32),
    )
    outs = pl.pallas_call(
        functools.partial(kernel, layers),
        out_shape=shapes,
        in_specs=[anywhere] * 9,
        out_specs=(pl.BlockSpec(memory_space=pltpu.VMEM),) * 3,
        scratch_shapes=[
            pltpu.VMEM(dinv_local.shape[1:], bf16),
            pltpu.VMEM(lower_anc.shape[1:], bf16),
            pltpu.VMEM(lower_high.shape[1:], bf16),
            pltpu.VMEM(rhs_anc.shape, f32),
            pltpu.VMEM(rhs_high.shape, f32),
            pltpu.VMEM((anc_order // anc_rows // CORES, CORES, anc_rows, anc_order), bf16),
            pltpu.VMEM(lower_anc_high.shape, bf16),
            pltpu.VMEM((supers, order, width), bf16),
            pltpu.VMEM((supers, order, width), bf16),
            pltpu.VMEM((anc_order, width), bf16),
            pltpu.VMEM((held + 1, BLOCK, width), f32),
            pltpu.VMEM((lower_high.shape[2], width), f32),
            pltpu.VMEM((2, BLOCK, anc_order), bf16),
            pltpu.VMEM((8, BLOCK, width), bf16),
            pltpu.VMEM((8, BLOCK, width), bf16),
            pltpu.VMEM((8, BLOCK, width), bf16),
            pltpu.VMEM((8, BLOCK, width), bf16),
            pltpu.VMEM((3, anc_rows, width), bf16),
            pltpu.VMEM((3, anc_rows, width), bf16),
            pltpu.VMEM((2, anc_rows, width), bf16),
            pltpu.SMEM(row_blocks.shape, jnp.int32),
            pltpu.SMEM((held,), jnp.int32),
            pltpu.SMEM((HBLK,), jnp.int32),
            pltpu.SemaphoreType.DMA((256,)),
            pltpu.SemaphoreType.DMA((256,)),
            pltpu.SemaphoreType.DMA((12,)),
            pltpu.SemaphoreType.REGULAR((2,)),
        ],
        compiler_params=pltpu.CompilerParams(collective_id=0, has_side_effects=True, vmem_limit_bytes=24 << 20),
    )(*[pltpu.with_memory_space_constraint(a, pltpu.HBM) for a in (row_blocks, rhs_local, dinv_local, lower_anc, lower_high, rhs_anc, rhs_high, dinv_anc, lower_anc_high)])
    return pl.pallas_call(
        hand_over,
        out_shape=shapes,
        in_specs=[pl.BlockSpec(memory_space=pltpu.VMEM)] * 3,
        out_specs=(anywhere,) * 3,
        scratch_shapes=[pltpu.SemaphoreType.DMA((3,))],
        compiler_params=pltpu.CompilerParams(vmem_limit_bytes=4 << 20),
    )(*outs)


def solution(mesh):
    return jax.shard_map(
        functools.partial(on_device, mesh.shape["layer"]),
        mesh=mesh,
        in_specs=(
            P("layer", None, "row", None),
            P("layer", None, "row", None),
            P("layer", None, "row", None),
            P("layer", None, "row", None),
            P("layer", None, "row"),
            P("row", None),
            P(("row", "layer"), None),
            P("row", None),
            P(("row", "layer"), None),
        ),
        out_specs=(P("layer", None, "row", None), P("row", None), P(("row", "layer"), None)),
        check_vma=False,
    )
```
